512 devices in a mesh: group: 64 (over y_lo, z, core), tp: 8 (over y_hi, x).
Axes of the slice: x: 4, y: 8 (y_hi: 2, y_lo: 4; y = y_hi * 4 + y_lo), z: 8, core: 2. Of those that a mesh axis runs over, the one named last changes fastest.
Arguments:
- tokens: bfloat16 [16384, 1024], P(('group', 'tp')), may hold values from -6 to 6
- variate: int32 [16384], P('group'), may hold values from 0 to 3
- time_ids: int32 [16384], P('group'), may hold values from 0 to 63
- cache_var: int32 [32768], P('group'), may hold values from 0 to 3
- cache_len: int32 [64], P('group'), may hold values from 1 to 512, as said below
- linked: int32 [64], P('group'), may hold values from 0 to 1, as said below
- cache_kv: bfloat16 [2, 32768, 1024], P(None, 'group', 'tp'), as said below
- var_bias: float32 [2, 16], P(None, 'tp'), may hold values from -2 to 2
- w_qkv: bfloat16 [3, 1024, 1024], P(None, None, 'tp'), may hold values from -0.1875 to 0.1875
- w_out: bfloat16 [1024, 1024], P('tp'), may hold values from -0.75 to 0.75
- w_gate_up: bfloat16 [2, 1024, 4096], P(None, None, 'tp'), may hold values from -0.1875 to 0.1875
- w_down: bfloat16 [4096, 1024], P('tp'), may hold values from -0.09375 to 0.09375
Outputs:
- layer_out: bfloat16 [16384, 1024], P(('group', 'tp'))
The draws below stay inside these ranges and needn't reach their ends.
Inputs may be any that keep to these rules, and one draw needn't show every extreme that they name: Group g's cached prefix fills its first cache_len[g] slots; some group has all 512. linked[g] equals linked[g + 32]; groups 0 and 32 are linked, and some other pair is not. `cache_kv`: cached keys already rotated, and cached values.
All inputs are finite; a program needn't handle non-finite values.
Results may differ from the reference program's by a relative error of at most 0.023.
Values may be sent and summed in bfloat16 or wider, within the bound.
A program may use at most 64 MiB of HBM per device.

```python
import jax
import jax.numpy as jnp
from jax import lax

D = 1024
H = 16
HD = 64
FF = 4096
TOK_GRP = 256
CACHE = 512
GROUPS = 64
TOKENS = 16384


def draw_cache_len(key, part):
    first_key, second_key, third_key = jax.random.split(key, 3)
    shift_by = jax.random.randint(first_key, (GROUPS,), 0, 4)
    top_value = jnp.right_shift(jnp.full((GROUPS,), CACHE, jnp.int32), shift_by)
    cut_value = jax.random.randint(second_key, (GROUPS,), 0, 1 << 20) % (top_value // 2 + 1)
    lengths = jnp.maximum(top_value - cut_value, 1)
    place_at = jax.random.randint(third_key, (), 0, GROUPS)
    return jnp.where(jnp.arange(GROUPS) == place_at, CACHE, lengths).astype(jnp.int32)


def draw_linked(key, part):
    first_key, second_key = jax.random.split(key, 2)
    half_count = GROUPS // 2
    flags = jax.random.randint(first_key, (half_count,), 0, 2)
    second_pos = 1 + jax.random.randint(second_key, (), 0, half_count - 1)
    positions = jnp.arange(half_count)
    flags = jnp.where(positions == 0, 1, jnp.where(positions == second_pos, 0, flags))
    return jnp.concatenate([flags, flags]).astype(jnp.int32)


def draw_cache_kv(key, part):
    base_draw = jax.random.normal(key, (2, GROUPS * CACHE, H * HD), jnp.float32)
    return base_draw.astype(jnp.bfloat16)


def place_ends(entries, rng, least, largest):
    spot = [jax.random.randint(jax.random.fold_in(rng, axis), (), 0, length) for axis, length in enumerate(entries.shape)]
    main_axis = entries.shape.index(max(entries.shape))
    beside = spot[:main_axis] + [(spot[main_axis] + 1) % entries.shape[main_axis]] + spot[main_axis + 1:]
    return entries.at[tuple(spot)].set(least).at[tuple(beside)].set(largest)


def steps_of(own_key, dims, cuts, low, high):
    def one(dim, shards_of):
        heights = jax.random.uniform(jax.random.fold_in(jax.random.fold_in(own_key, 6), dim), (shards_of,), jnp.float32, low / len(cuts), high / len(cuts))
        return jnp.repeat(jnp.exp(heights), dims[dim] // shards_of).reshape((-1,) + (1,) * (len(dims) - dim - 1))

    factor_of = one(*cuts[0])
    for cut in cuts[1:]:
        factor_of = factor_of * one(*cut)
    return factor_of


def scatter_about(own_key, extent, width, bound, shards=(), held_as=jnp.bfloat16):
    level = steps_of(own_key, extent, shards, -0.22, 0.18) if shards else 1.0
    result = jax.random.normal(own_key, extent, jnp.float32) * width * level
    return jnp.minimum(jnp.maximum(result, -bound), bound).astype(held_as)


def setup_inputs(seed: int = 0) -> dict:
    key_of = jax.random.split(jax.random.key(seed), 13)
    tokens = scatter_about(key_of[0], (TOKENS, D), 1.0, 6.0, ((0, 512),))
    variate = place_ends(jax.random.randint(key_of[1], (TOKENS,), 0, 4), jax.random.fold_in(key_of[1], 1), 0, 3).astype(jnp.int32)
    time_ids = place_ends(jax.random.randint(key_of[2], (TOKENS,), 0, TOK_GRP // 4), jax.random.fold_in(key_of[2], 1), 0, (TOK_GRP // 4) - 1).astype(jnp.int32)
    cache_var = place_ends(jax.random.randint(key_of[3], (GROUPS * CACHE,), 0, 4), jax.random.fold_in(key_of[3], 1), 0, 3).astype(jnp.int32)
    cache_len = draw_cache_len(jax.random.fold_in(key_of[12], 71), 0)
    linked = draw_linked(jax.random.fold_in(key_of[12], 71), 0)
    cache_kv = draw_cache_kv(jax.random.fold_in(key_of[12], 71), 0)
    var_bias = jnp.clip(jax.random.uniform(key_of[7], (2, H), jnp.float32, -2.0, 2.0) * steps_of(key_of[7], (2, H), ((1, 8),), -0.4, 0.0), -2.0, 2.0)
    w_qkv = scatter_about(key_of[8], (3, D, H * HD), D ** -0.5, 0.1875, ((2, 8),))
    w_out = scatter_about(key_of[9], (H * HD, D), HD ** -0.5, 0.75, ((0, 8),))
    w_gate_up = scatter_about(key_of[10], (2, D, FF), D ** -0.5, 0.1875, ((2, 8),))
    w_down = scatter_about(key_of[11], (FF, D), FF ** -0.5, 0.09375, ((0, 8),))
    return {"tokens": tokens, "variate": variate, "time_ids": time_ids, "cache_var": cache_var, "cache_len": cache_len, "linked": linked, "cache_kv": cache_kv, "var_bias": var_bias, "w_qkv": w_qkv, "w_out": w_out, "w_gate_up": w_gate_up, "w_down": w_down}


far_future = 1073741824
masked_score = -1e+30

def normed(row_block):
    values = row_block.astype(jnp.float32)
    return values * lax.rsqrt(lax.optimization_barrier(jnp.mean(values * values, axis=-1, keepdims=True)) + 1e-05)

def rotary(values, position, head_count):
    row_count = values.shape[0]
    shaped = values.reshape(row_count, head_count, -1)
    half_width = shaped.shape[-1] // 2
    frequency = 10000.0 ** (-jnp.arange(half_width, dtype=jnp.float32) / half_width)
    angles = position.astype(jnp.float32)[:, None] * frequency[None, :]
    cosine = jnp.cos(angles)[:, None, :]
    sine_part = jnp.sin(angles)[:, None, :]
    lower_half = shaped[..., :half_width]
    upper_half = shaped[..., half_width:]
    turned = jnp.concatenate([lower_half * cosine - upper_half * sine_part, upper_half * cosine + lower_half * sine_part], axis=-1)
    return turned.reshape(row_count, -1)

def reference(tokens, variate, time_ids, cache_var, cache_len, linked, cache_kv, var_bias, w_qkv, w_out, w_gate_up, w_down):
    head_count = var_bias.shape[1]
    normal_in = normed(tokens).astype(jnp.bfloat16)
    projected = jnp.stack([jnp.dot(normal_in, w_qkv[part_index], preferred_element_type=jnp.float32) for part_index in range(3)])
    queries = rotary(projected[0], time_ids, head_count).astype(jnp.bfloat16)
    new_keys = rotary(projected[1], time_ids, head_count).astype(jnp.bfloat16)
    new_vals = projected[2].astype(jnp.bfloat16)
    new_kv = jnp.stack([new_keys, new_vals])

    def key_set(group_id):
        cache_part = lax.dynamic_slice_in_dim(cache_kv, group_id * CACHE, CACHE, 1)
        new_part = lax.dynamic_slice_in_dim(new_kv, group_id * TOK_GRP, TOK_GRP, 1)
        slot_ids = jnp.arange(CACHE, dtype=jnp.int32)
        cache_time = jnp.where(slot_ids < cache_len[group_id], -1, far_future).astype(jnp.int32)
        new_time = lax.dynamic_slice_in_dim(time_ids, group_id * TOK_GRP, TOK_GRP, 0).astype(jnp.int32)
        key_time = jnp.concatenate([cache_time, new_time])
        key_var = jnp.concatenate([lax.dynamic_slice_in_dim(cache_var, group_id * CACHE, CACHE, 0).astype(jnp.int32), lax.dynamic_slice_in_dim(variate, group_id * TOK_GRP, TOK_GRP, 0).astype(jnp.int32)])
        return (jnp.concatenate([cache_part, new_part], axis=1), key_time, key_var)

    def one_group(group_id):
        partner_id = jnp.bitwise_xor(group_id, GROUPS // 2).astype(jnp.int32)
        own_kv, own_time, own_var = key_set(group_id)
        far_kv, far_time, far_var = key_set(partner_id)
        far_time = jnp.where(linked[group_id] > 0, far_time, far_future).astype(jnp.int32)
        key_vals = jnp.concatenate([own_kv, far_kv], axis=1)
        key_time = jnp.concatenate([own_time, far_time])
        key_var = jnp.concatenate([own_var, far_var])
        query_rows = lax.dynamic_slice_in_dim(queries, group_id * TOK_GRP, TOK_GRP, 0)
        query_time = lax.dynamic_slice_in_dim(time_ids, group_id * TOK_GRP, TOK_GRP, 0)
        query_var = lax.dynamic_slice_in_dim(variate, group_id * TOK_GRP, TOK_GRP, 0)
        query_heads = query_rows.reshape(TOK_GRP, head_count, -1).astype(jnp.float32)
        key_heads = key_vals[0].reshape(key_vals.shape[1], head_count, -1).astype(jnp.float32)
        value_heads = key_vals[1].reshape(key_vals.shape[1], head_count, -1).astype(jnp.float32)
        scores = jnp.einsum('thd,khd->htk', query_heads, key_heads) * 0.125
        same_variate = (query_var[:, None] == key_var[None, :])[None]
        scores = scores + jnp.where(same_variate, var_bias[0][:, None, None], var_bias[1][:, None, None])
        visible = (key_time[None, :] <= query_time[:, None])[None]
        scores = jnp.where(visible, scores, masked_score)
        row_best = lax.optimization_barrier(jnp.max(scores, axis=-1, keepdims=True))
        weights = jnp.exp(scores - row_best)
        denom = lax.optimization_barrier(jnp.sum(weights, axis=-1))
        rounded = lax.optimization_barrier(weights.astype(jnp.bfloat16)).astype(jnp.float32)
        attended = jnp.einsum('htk,khd->htd', rounded, value_heads) / denom[..., None]
        return attended.transpose(1, 0, 2).reshape(TOK_GRP, -1).astype(jnp.bfloat16)
    attn_heads = lax.map(one_group, jnp.arange(GROUPS, dtype=jnp.int32)).reshape(TOKENS, -1)
    stream = (tokens.astype(jnp.float32) + jnp.dot(attn_heads, w_out, preferred_element_type=jnp.float32)).astype(jnp.bfloat16)
    normed_mid = normed(stream).astype(jnp.bfloat16)
    gate_part = jnp.dot(normed_mid, w_gate_up[0], preferred_element_type=jnp.float32)
    up_part = jnp.dot(normed_mid, w_gate_up[1], preferred_element_type=jnp.float32)
    hidden = (jax.nn.silu(gate_part) * up_part).astype(jnp.bfloat16)
    ffn_out = jnp.dot(hidden, w_down, preferred_element_type=jnp.float32)
    return (stream.astype(jnp.float32) + ffn_out).astype(jnp.bfloat16)
```

```python
import jax
import jax.numpy as jnp
from jax import lax
from jax.experimental import pallas as pl
from jax.experimental.pallas import tpu as pltpu
from jax.sharding import PartitionSpec as P

F32 = jnp.float32
BF16 = jnp.bfloat16
MASKED = -1e30
GROUPS = 64
TP = 8
XN = 4
ROWS = 32
TOK = 256
HALF = 128
CACHE = 512
KEYS = CACHE + TOK
D = 1024
HW = 128
HD = 64
FF = 512

TY, TX, TF, ME, QQ, O1, O2, AX, W1, W2, W3, W4, RF, RN, RY, NSEM = (
    0, 1, 4, 7, 8, 9, 11, 15, 18, 19, 22, 25, 29, 32, 35, 36,
)


def dot(a, b):
    return jnp.dot(a, b, preferred_element_type=F32)


def normed(values):
    return values * lax.rsqrt(jnp.mean(values * values, axis=-1, keepdims=True) + 1e-05)


def spread(row):
    return jnp.broadcast_to(row, (HW, row.shape[1])).T


def layer(
    tok, tim, var, cvar, clen, lnk, ckv, vb, wqkv, wo, wgu, wd,
    out,
    x_all, wq, ke, vn, vt, qs, qe, qr, qe2, me_s, me_r, cvr, cs, sn,
    o1s, s1s, o1r, s1r, o2s, s2s, o2r, s2r,
    a3, wof, wguv, wdv, st, hid, far, near, rf, rn, ys, yr,
    ssem, rsem, lsem,
):
    g = lax.axis_index("group")
    t = lax.axis_index("tp")
    x = lax.rem(t, XN)
    yh = lax.div(t, XN)
    core = lax.rem(g, 2)
    t_far = lax.rem(t + XN, TP)
    g_par = lax.rem(g + GROUPS // 2, GROUPS)
    g_sib = g + 1 - 2 * core

    def xpeer(k):
        return (g, yh * XN + lax.rem(x + k, XN))

    ypeer = (g, t_far)
    ppeer = (g_par, t)
    fpeer = (g_par, t_far)
    speer = (g_sib, t)

    def remote(slot, src, dst, peer):
        return pltpu.make_async_remote_copy(
            src_ref=src, dst_ref=dst, send_sem=ssem.at[slot], recv_sem=rsem.at[slot],
            device_id=peer, device_id_type=pl.DeviceIdType.MESH,
        )

    barrier = pltpu.get_barrier_semaphore()
    for peer in (ypeer, ppeer, fpeer, speer, xpeer(1), xpeer(2), xpeer(3)):
        pl.semaphore_signal(barrier, inc=1, device_id=peer, device_id_type=pl.DeviceIdType.MESH)

    own_rows = pl.ds(pl.multiple_of(t * ROWS, ROWS), ROWS)
    far_rows = pl.ds(pl.multiple_of(t_far * ROWS, ROWS), ROWS)

    def local(slot, src, dst):
        copy = pltpu.make_async_copy(src, dst, lsem.at[slot])
        copy.start()
        return copy

    ld_tok = local(0, tok, x_all.at[own_rows])
    ld_tim = local(1, tim, me_s.at[pl.ds(0, 1)])
    ld_var = local(2, var, me_s.at[pl.ds(1, 1)])
    ld_cvar = local(3, cvar, cvr)
    ld_w = [local(4 + c, wqkv.at[c], wq.at[:, pl.ds(c * HW, HW)]) for c in range(3)]
    ld_k = local(7, ckv.at[0], ke.at[pl.ds(0, CACHE), pl.ds(0, HW)])
    ld_v = local(8, ckv.at[1], vn)
    ld_wo = [local(9 + c, wo.at[pl.ds(c * HD, HD)], wof.at[x, yh, c]) for c in range(2)]
    ld_gu = [local(11 + c, wgu.at[c], wguv.at[:, pl.ds(c * FF, FF)]) for c in range(2)]
    ld_d = local(13, wd, wdv)
    ld_tok.wait()
    ld_tim.wait()
    ld_var.wait()
    pl.semaphore_wait(barrier, 7)

    tok_y = remote(TY, x_all.at[own_rows], x_all.at[own_rows], ypeer)
    tok_y.start()
    tok_x = [remote(TX + k, x_all.at[own_rows], x_all.at[own_rows], xpeer(k + 1)) for k in range(3)]
    for copy in tok_x:
        copy.start()
    meta = remote(ME, me_s, me_r, ppeer)
    meta.start()

    time_row = me_s[0:1, :].astype(F32)
    var_row = me_s[1:2, :].astype(F32)
    freq = jnp.exp(
        lax.broadcasted_iota(jnp.int32, (HD // 2, TOK), 0).astype(F32) * (-9.210340371976184 / 32)
    )
    angle = freq * time_row
    cs[...] = jnp.cos(angle)
    sn[...] = jnp.sin(angle)

    lane = lax.broadcasted_iota(jnp.int32, (CACHE, HW), 1)
    slot = lax.broadcasted_iota(jnp.int32, (CACHE, HW), 0)
    lane_var = lax.rem(lane, 4).astype(F32)
    in_var = (lane >= HD) & (lane < HD + 12)
    ld_cvar.wait()
    same = jnp.where(spread(cvr[...].astype(F32)) == lane_var, 1.0, 0.0)
    shut = jnp.where(slot >= clen[0], MASKED, 0.0)
    ke[0:CACHE, HW:] = jnp.where(lane < HD, shut, jnp.where(in_var, same, 0.0)).astype(BF16)
    lane = lane[:TOK]
    same = jnp.where(spread(var_row) == lane_var[:TOK], 1.0, 0.0)
    shut = jnp.where(spread(time_row) > lane.astype(F32), MASKED, 0.0)
    ke[CACHE:, HW:] = jnp.where(lane < HD, shut, jnp.where(in_var[:TOK], same, 0.0)).astype(BF16)

    def query_side(dst, times, variates):
        row = lax.broadcasted_iota(jnp.int32, (HD, TOK), 0)
        at_time = jnp.where(row.astype(F32) == times, 1.0, 0.0).astype(BF16)
        hit = lax.rem(row, 4).astype(F32) == variates
        for h in range(2):
            bias = jnp.where(hit, vb[0, h], vb[1, h])
            high = bias.astype(BF16).astype(F32)
            mid = (bias - high).astype(BF16).astype(F32)
            low = bias - high - mid
            parts = jnp.where(
                row < 4, high, jnp.where(row < 8, mid, jnp.where(row < 12, low, 0.0))
            )
            dst[h, HW : HW + HD, :] = at_time
            dst[h, HW + HD :, :] = parts.astype(BF16)
            dst[h, (1 - h) * HD : (2 - h) * HD, :] = jnp.zeros((HD, TOK), BF16)

    query_side(qe, time_row, var_row)
    ld_v.wait()
    vt[:, 0:CACHE] = vn[...].astype(F32).T.astype(BF16)
    for copy in ld_w:
        copy.wait()
    for copy in ld_wo:
        copy.wait()

    tok_y.wait_send()
    w1 = remote(W1, wof.at[x, yh, core], wof.at[x, yh, core], ypeer)
    w1.start()

    def qkv(half):
        base = pl.multiple_of(half * HALF, HALF)
        rows = pl.ds(base, HALF)
        normal = normed(x_all[rows, :].astype(F32)).astype(BF16)
        prod = dot(normal, wq[...])
        cosine = cs[:, rows]
        sine = sn[:, rows]

        def turned(u):
            parts = []
            for h in range(2):
                lo = u[h * HD : h * HD + HD // 2]
                hi = u[h * HD + HD // 2 : (h + 1) * HD]
                parts += [lo * cosine - hi * sine, hi * cosine + lo * sine]
            return jnp.concatenate(parts, axis=0)

        q = turned(prod[:, 0:HW].T).astype(BF16).astype(F32) * 0.125
        qs[:, rows] = q.astype(BF16)
        k = turned(prod[:, HW : 2 * HW].T)
        v = prod[:, 2 * HW :].T
        new = pl.ds(pl.multiple_of(base + CACHE, HALF), HALF)
        return (new, k, v)

    def keep(new, k, v):
        ke[new, 0:HW] = k.T.astype(BF16)
        vt[:, new] = v.astype(BF16)

    tok_y.wait_recv()
    tok_f = [remote(TF + k, x_all.at[far_rows], x_all.at[far_rows], xpeer(k + 1)) for k in range(3)]
    for copy in tok_f:
        copy.start()
    for copy in tok_x:
        copy.wait_recv()
    keep(*qkv(yh))
    w2 = [remote(W2 + k, wof.at[x, yh, core], wof.at[x, yh, core], xpeer(k + 1)) for k in range(3)]
    for copy in w2:
        copy.start()
    for copy in tok_f:
        copy.wait_recv()
    rest = qkv(1 - yh)
    send_q = remote(QQ, qs, qr, ppeer)
    send_q.start()
    keep(*rest)
    ld_k.wait()

    def attend(dst, h):
        s = dot(ke[...], dst[h])
        best = jnp.max(s, axis=0, keepdims=True)
        p = jnp.exp(s - best)
        total = jnp.sum(p, axis=0, keepdims=True)
        o = dot(vt[h * HD : (h + 1) * HD, :], p.astype(BF16))
        return o, best, total

    def both_heads(dst, q, o_ref, s_ref):
        s_ref[...] = jnp.zeros(s_ref.shape, F32)
        for h in range(2):
            dst[h, h * HD : (h + 1) * HD, :] = q[h * HD : (h + 1) * HD, :]
            o, best, total = attend(dst, h)
            o_ref[h * HD : (h + 1) * HD, :] = o.astype(BF16)
            s_ref[h : h + 1, :] = best
            s_ref[2 + h : 3 + h, :] = total

    both_heads(qe, qs, o1s, s1s)
    send_o1 = [remote(O1, o1s, o1r, ypeer), remote(O1 + 1, s1s, s1r, ypeer)]
    for copy in send_o1:
        copy.start()

    meta.wait_recv()
    query_side(qe2, me_r[0:1, :].astype(F32), me_r[1:2, :].astype(F32))
    send_q.wait_recv()
    both_heads(qe2, qr, o2s, s2s)
    send_o2 = [
        remote(O2, o2s, o2r.at[0], ppeer), remote(O2 + 1, s2s, s2r.at[0], ppeer),
        remote(O2 + 2, o2s, o2r.at[1], fpeer), remote(O2 + 3, s2s, s2r.at[1], fpeer),
    ]
    for copy in send_o2:
        copy.start()

    yf = 1 - yh
    w1.wait_recv()
    w3 = [remote(W3 + k, wof.at[x, yf, core], wof.at[x, yf, core], xpeer(k + 1)) for k in range(3)]
    for copy in w3:
        copy.start()
    w4 = [remote(W4, wof.at[x, yf, core], wof.at[x, yf, core], speer)]
    w4[0].start()

    def merged(o_a, s_a, o_b, s_b):
        on = lnk[0] > 0
        parts = []
        for h in range(2):
            head = slice(h * HD, (h + 1) * HD)
            m_a = s_a[h : h + 1, :]
            m_b = jnp.where(on, s_b[h : h + 1, :], MASKED)
            best = jnp.maximum(m_a, m_b)
            f_a = jnp.exp(m_a - best)
            f_b = jnp.where(on, jnp.exp(m_b - best), 0.0)
            total = f_a * s_a[2 + h : 3 + h, :] + f_b * s_b[2 + h : 3 + h, :]
            parts.append(
                (f_a * o_a[head, :].astype(F32) + f_b * o_b[head, :].astype(F32)) / total
            )
        return jnp.concatenate(parts, axis=0).T

    for copy in send_o1:
        copy.wait_recv()
    for copy in send_o2:
        copy.wait_recv()
    mine = merged(o1s, s1s, o2r.at[0], s2r.at[0])
    other = merged(o1r, s1r, o2r.at[1], s2r.at[1])
    a3[x, :, 0:HW] = jnp.where(yh == 0, mine, other).astype(BF16)
    a3[x, :, HW:] = jnp.where(yh == 0, other, mine).astype(BF16)
    send_a = [remote(AX + k, a3.at[x], a3.at[x], xpeer(k + 1)) for k in range(3)]
    for copy in send_a:
        copy.start()

    for k in range(3):
        w2[k].wait_recv()
        w3[k].wait_recv()
        xk = lax.rem(x + 3 - k, XN)
        copy = remote(W4 + 1 + k, wof.at[xk, :, core], wof.at[xk, :, core], speer)
        copy.start()
        w4.append(copy)

    for copy in w4:
        copy.wait_recv()
    st[...] = x_all[...].astype(F32)
    st[...] += dot(a3[x], wof[x].reshape(2 * HW, D))
    for k in (0, 2, 1):
        send_a[k].wait_recv()
        xk = lax.rem(x + 3 - k, XN)
        st[...] += dot(a3[xk], wof[xk].reshape(2 * HW, D))

    for copy in ld_gu:
        copy.wait()
    ld_d.wait()
    for half in range(2):
        rows = slice(half * HALF, (half + 1) * HALF)
        stream = st[rows, :].astype(BF16).astype(F32)
        st[rows, :] = stream
        gate_up = dot(normed(stream).astype(BF16), wguv[...])
        gate = gate_up[:, :FF]
        hid[rows, :] = (gate / (1.0 + jnp.exp(-gate)) * gate_up[:, FF:]).astype(BF16)

    def down(half, dst):
        dst[...] = dot(hid[pl.ds(pl.multiple_of(half * HALF, HALF), HALF), :], wdv[...]).astype(BF16)

    def block(k):
        return pl.ds(pl.multiple_of(lax.rem(x + k, XN) * ROWS, ROWS), ROWS)

    down(yf, far)
    send_f = [remote(RF + k, far.at[block(k + 1)], rf.at[k], xpeer(k + 1)) for k in range(3)]
    for copy in send_f:
        copy.start()
    down(yh, near)
    send_n = [remote(RN + k, near.at[block(k + 1)], rn.at[k], xpeer(k + 1)) for k in range(3)]
    for copy in send_n:
        copy.start()
    total = far[block(0), :].astype(F32)
    for k in range(3):
        send_f[k].wait_recv()
        total = total + rf[k].astype(F32)
    ys[...] = total.astype(BF16)
    send_y = remote(RY, ys, yr, ypeer)
    send_y.start()
    total = near[block(0), :].astype(F32)
    for k in range(3):
        send_n[k].wait_recv()
        total = total + rn[k].astype(F32)
    total = total + st[own_rows, :]
    for copy in [tok_y][:0] + tok_x + tok_f + [meta, w1, send_q] + w2 + w3 + w4 + send_o1 + send_o2 + send_a:
        copy.wait_send()
    for copy in send_f + send_n:
        copy.wait_send()
    send_y.wait_recv()
    out[...] = (total + yr[...].astype(F32)).astype(BF16)
    send_y.wait_send()


def shards(
    tokens, variate, time_ids, cache_var, cache_len, linked, cache_kv, var_bias,
    w_qkv, w_out, w_gate_up, w_down,
):
    anyspace = pl.BlockSpec(memory_space=pl.ANY)
    smem = pl.BlockSpec(memory_space=pltpu.SMEM)
    vmem = pltpu.VMEM
    scratch = [
        vmem((TOK, D), BF16),
        vmem((D, 3 * HW), BF16),
        vmem((KEYS, 2 * HW), BF16),
        vmem((CACHE, HW), BF16),
        vmem((HW, KEYS), BF16),
        vmem((HW, TOK), BF16),
        vmem((2, 2 * HW, TOK), BF16),
        vmem((HW, TOK), BF16),
        vmem((2, 2 * HW, TOK), BF16),
        vmem((2, TOK), jnp.int32),
        vmem((2, TOK), jnp.int32),
        vmem((1, CACHE), jnp.int32),
        vmem((HD // 2, TOK), F32),
        vmem((HD // 2, TOK), F32),
        vmem((HW, TOK), BF16), vmem((8, TOK), F32),
        vmem((HW, TOK), BF16), vmem((8, TOK), F32),
        vmem((HW, TOK), BF16), vmem((8, TOK), F32),
        vmem((2, HW, TOK), BF16), vmem((2, 8, TOK), F32),
        vmem((XN, TOK, 2 * HW), BF16),
        vmem((XN, 2, 2, HD, D), BF16),
        vmem((D, 2 * FF), BF16),
        vmem((FF, D), BF16),
        vmem((TOK, D), F32),
        vmem((TOK, FF), BF16),
        vmem((HALF, D), BF16),
        vmem((HALF, D), BF16),
        vmem((3, ROWS, D), BF16),
        vmem((3, ROWS, D), BF16),
        vmem((ROWS, D), BF16),
        vmem((ROWS, D), BF16),
        pltpu.SemaphoreType.DMA((NSEM,)),
        pltpu.SemaphoreType.DMA((NSEM,)),
        pltpu.SemaphoreType.DMA((14,)),
    ]
    return pl.pallas_call(
        layer,
        out_shape=jax.ShapeDtypeStruct((ROWS, D), BF16),
        in_specs=[
            anyspace, anyspace, anyspace, anyspace, smem, smem, anyspace, smem,
            anyspace, anyspace, anyspace, anyspace,
        ],
        out_specs=pl.BlockSpec(memory_space=pltpu.VMEM),
        scratch_shapes=scratch,
        compiler_params=pltpu.CompilerParams(
            collective_id=0, has_side_effects=True, vmem_limit_bytes=48 << 20
        ),
        name="layer",
    )(
        tokens, time_ids.reshape(1, TOK), variate.reshape(1, TOK), cache_var.reshape(1, CACHE),
        cache_len, linked, cache_kv, var_bias, w_qkv, w_out, w_gate_up, w_down,
    )


def solution(mesh):
    return jax.shard_map(
        shards,
        mesh=mesh,
        in_specs=(
            P(("group", "tp"), None),
            P("group"),
            P("group"),
            P("group"),
            P("group"),
            P("group"),
            P(None, "group", "tp"),
            P(None, "tp"),
            P(None, None, "tp"),
            P("tp", None),
            P(None, None, "tp"),
            P("tp", None),
        ),
        out_specs=P(("group", "tp"), None),
        check_vma=False,
    )
```

```python
import jax
import jax.numpy as jnp
from jax import lax
from jax.experimental import pallas as pl
from jax.experimental.pallas import tpu as pltpu
from jax.sharding import PartitionSpec as P

F32 = jnp.float32
BF16 = jnp.bfloat16
MASKED = -1e30
GROUPS = 64
TP = 8
XN = 4
ROWS = 32
TOK = 256
HALF = 128
CACHE = 512
KEYS = CACHE + TOK
D = 1024
HW = 128
HD = 64
FF = 512

TY, TX, TF, ME, QQ, O1, O2, AX, W1, W2, W3, W4, RF, RN, RY, NSEM = (
    0, 1, 4, 7, 8, 9, 11, 15, 18, 19, 22, 25, 29, 32, 35, 36,
)


def dot(a, b):
    return jnp.dot(a, b, preferred_element_type=F32)


def normed(values):
    return values * lax.rsqrt(jnp.mean(values * values, axis=-1, keepdims=True) + 1e-05)


def spread(row):
    return jnp.broadcast_to(row, (HW, row.shape[1])).T


def layer(
    tok, tim, var, cvar, clen, lnk, ckv, vb, wqkv, wo, wgu, wd,
    out,
    x_all, wq, ke, vn, vt, qs, qe, qr, qe2, me_s, me_r, cvr, cs, sn,
    o1s, s1s, o1r, s1r, o2s, s2s, o2r, s2r,
    a3, wof, wguv, wdv, st, hid, far, near, rf, rn, ys, yr,
    ssem, rsem, lsem,
):
    g = lax.axis_index("group")
    t = lax.axis_index("tp")
    x = lax.rem(t, XN)
    yh = lax.div(t, XN)
    core = lax.rem(g, 2)
    t_far = lax.rem(t + XN, TP)
    g_par = lax.rem(g + GROUPS // 2, GROUPS)
    g_sib = g + 1 - 2 * core

    def xpeer(k):
        return (g, yh * XN + lax.rem(x + k, XN))

    ypeer = (g, t_far)
    ppeer = (g_par, t)
    fpeer = (g_par, t_far)
    speer = (g_sib, t)

    def remote(slot, src, dst, peer):
        return pltpu.make_async_remote_copy(
            src_ref=src, dst_ref=dst, send_sem=ssem.at[slot], recv_sem=rsem.at[slot],
            device_id=peer, device_id_type=pl.DeviceIdType.MESH,
        )

    loads = []
    loaded = []
    started = []
    arrived = []

    def go(*copies):
        for copy in copies:
            copy.start()
            started.append(copy)

    def arrive(*copies):
        for copy in copies:
            copy.wait_recv()
            arrived.append(copy)

    barrier = pltpu.get_barrier_semaphore()
    for peer in (ypeer, ppeer, fpeer, speer, xpeer(1), xpeer(2), xpeer(3)):
        pl.semaphore_signal(barrier, inc=1, device_id=peer, device_id_type=pl.DeviceIdType.MESH)

    own_rows = pl.ds(pl.multiple_of(t * ROWS, ROWS), ROWS)
    far_rows = pl.ds(pl.multiple_of(t_far * ROWS, ROWS), ROWS)

    def local(slot, src, dst):
        copy = pltpu.make_async_copy(src, dst, lsem.at[slot])
        copy.start()
        loads.append(copy)
        return copy

    def ready(*copies):
        for copy in copies:
            copy.wait()
            loaded.append(copy)

    ld_tok = local(0, tok, x_all.at[own_rows])
    ld_tim = local(1, tim, me_s.at[pl.ds(0, 1)])
    ld_var = local(2, var, me_s.at[pl.ds(1, 1)])
    ld_cvar = local(3, cvar, cvr)
    ld_w = [local(4 + c, wqkv.at[c], wq.at[:, pl.ds(c * HW, HW)]) for c in range(3)]
    ld_k = local(7, ckv.at[0], ke.at[pl.ds(0, CACHE), pl.ds(0, HW)])
    ld_v = local(8, ckv.at[1], vn)
    ld_wo = [local(9 + c, wo.at[pl.ds(c * HD, HD)], wof.at[x, yh, c]) for c in range(2)]
    ld_gu = [local(11 + c, wgu.at[c], wguv.at[:, pl.ds(c * FF, FF)]) for c in range(2)]
    ld_d = local(13, wd, wdv)
    ready(ld_tim)
    ready(ld_var)

    time_row = me_s[0:1, :].astype(F32)
    var_row = me_s[1:2, :].astype(F32)
    freq = jnp.exp(
        lax.broadcasted_iota(jnp.int32, (HD // 2, TOK), 0).astype(F32) * (-9.210340371976184 / 32)
    )
    angle = freq * time_row
    cs[...] = jnp.cos(angle)
    sn[...] = jnp.sin(angle)

    lane = lax.broadcasted_iota(jnp.int32, (CACHE, HW), 1)
    slot = lax.broadcasted_iota(jnp.int32, (CACHE, HW), 0)
    lane_var = lax.rem(lane, 4).astype(F32)
    in_var = (lane >= HD) & (lane < HD + 12)
    ready(ld_cvar)
    same = jnp.where(spread(cvr[...].astype(F32)) == lane_var, 1.0, 0.0)
    shut = jnp.where(slot >= clen[0], MASKED, 0.0)
    ke[0:CACHE, HW:] = jnp.where(lane < HD, shut, jnp.where(in_var, same, 0.0)).astype(BF16)
    lane = lane[:TOK]
    same = jnp.where(spread(var_row) == lane_var[:TOK], 1.0, 0.0)
    shut = jnp.where(spread(time_row) > lane.astype(F32), MASKED, 0.0)
    ke[CACHE:, HW:] = jnp.where(lane < HD, shut, jnp.where(in_var[:TOK], same, 0.0)).astype(BF16)

    def query_side(dst, times, variates):
        row = lax.broadcasted_iota(jnp.int32, (HD, TOK), 0)
        at_time = jnp.where(row.astype(F32) == times, 1.0, 0.0).astype(BF16)
        hit = lax.rem(row, 4).astype(F32) == variates
        for h in range(2):
            bias = jnp.where(hit, vb[0, h], vb[1, h])
            high = bias.astype(BF16).astype(F32)
            mid = (bias - high).astype(BF16).astype(F32)
            low = bias - high - mid
            parts = jnp.where(
                row < 4, high, jnp.where(row < 8, mid, jnp.where(row < 12, low, 0.0))
            )
            dst[h, HW : HW + HD, :] = at_time
            dst[h, HW + HD :, :] = parts.astype(BF16)
            dst[h, (1 - h) * HD : (2 - h) * HD, :] = jnp.zeros((HD, TOK), BF16)

    query_side(qe, time_row, var_row)
    ready(ld_v)
    vt[:, 0:CACHE] = vn[...].astype(F32).T.astype(BF16)
    ready(ld_tok)
    pl.semaphore_wait(barrier, 7)

    tok_y = remote(TY, x_all.at[own_rows], x_all.at[own_rows], ypeer)
    go(tok_y)
    tok_x = [remote(TX + k, x_all.at[own_rows], x_all.at[own_rows], xpeer(k + 1)) for k in range(3)]
    go(*tok_x)
    meta = remote(ME, me_s, me_r, ppeer)
    go(meta)

    ready(*ld_w)
    ready(*ld_wo)


    w1 = remote(W1, wof.at[x, yh, core], wof.at[x, yh, core], ypeer)
    go(w1)
    def qkv(half):
        base = pl.multiple_of(half * HALF, HALF)
        rows = pl.ds(base, HALF)
        normal = normed(x_all[rows, :].astype(F32)).astype(BF16)
        prod = dot(normal, wq[...])
        cosine = cs[:, rows]
        sine = sn[:, rows]

        def turned(u):
            parts = []
            for h in range(2):
                lo = u[h * HD : h * HD + HD // 2]
                hi = u[h * HD + HD // 2 : (h + 1) * HD]
                parts += [lo * cosine - hi * sine, hi * cosine + lo * sine]
            return jnp.concatenate(parts, axis=0)

        q = turned(prod[:, 0:HW].T).astype(BF16).astype(F32) * 0.125
        qs[:, rows] = q.astype(BF16)
        k = turned(prod[:, HW : 2 * HW].T)
        v = prod[:, 2 * HW :].T
        new = pl.ds(pl.multiple_of(base + CACHE, HALF), HALF)
        return (new, k, v)

    def keep(new, k, v):
        ke[new, 0:HW] = k.T.astype(BF16)
        vt[:, new] = v.astype(BF16)

    arrive(tok_y)
    tok_f = [remote(TF + k, x_all.at[far_rows], x_all.at[far_rows], xpeer(k + 1)) for k in range(3)]
    go(*tok_f)
    arrive(*tok_x)
    keep(*qkv(yh))
    w2 = [remote(W2 + k, wof.at[x, yh, core], wof.at[x, yh, core], xpeer(k + 1)) for k in range(3)]
    go(*w2)
    arrive(*tok_f)
    rest = qkv(1 - yh)
    send_q = remote(QQ, qs, qr, ppeer)
    go(send_q)
    keep(*rest)
    ready(ld_k)

    def attend(dst, h):
        s = dot(ke[...], dst[h])
        best = jnp.max(s, axis=0, keepdims=True)
        p = jnp.exp(s - best)
        total = jnp.sum(p, axis=0, keepdims=True)
        o = dot(vt[h * HD : (h + 1) * HD, :], p.astype(BF16))
        return o, best, total

    def both_heads(dst, q, o_ref, s_ref):
        s_ref[...] = jnp.zeros(s_ref.shape, F32)
        for h in range(2):
            dst[h, h * HD : (h + 1) * HD, :] = q[h * HD : (h + 1) * HD, :]
            o, best, total = attend(dst, h)
            o_ref[h * HD : (h + 1) * HD, :] = o.astype(BF16)
            s_ref[h : h + 1, :] = best
            s_ref[2 + h : 3 + h, :] = total

    both_heads(qe, qs, o1s, s1s)
    send_o1 = [remote(O1, o1s, o1r, ypeer), remote(O1 + 1, s1s, s1r, ypeer)]
    go(*send_o1)

    yf = 1 - yh
    arrive(w1)
    w3 = [remote(W3 + k, wof.at[x, yf, core], wof.at[x, yf, core], xpeer(k + 1)) for k in range(3)]
    go(*w3)
    w4 = [remote(W4, wof.at[x, yf, core], wof.at[x, yf, core], speer)]
    go(w4[0])
    arrive(meta)
    query_side(qe2, me_r[0:1, :].astype(F32), me_r[1:2, :].astype(F32))
    arrive(send_q)
    both_heads(qe2, qr, o2s, s2s)
    send_o2 = [
        remote(O2, o2s, o2r.at[0], ppeer), remote(O2 + 1, s2s, s2r.at[0], ppeer),
        remote(O2 + 2, o2s, o2r.at[1], fpeer), remote(O2 + 3, s2s, s2r.at[1], fpeer),
    ]
    go(*send_o2)


    def merged(o_a, s_a, o_b, s_b):
        on = lnk[0] > 0
        parts = []
        for h in range(2):
            head = slice(h * HD, (h + 1) * HD)
            m_a = s_a[h : h + 1, :]
            m_b = jnp.where(on, s_b[h : h + 1, :], MASKED)
            best = jnp.maximum(m_a, m_b)
            f_a = jnp.exp(m_a - best)
            f_b = jnp.where(on, jnp.exp(m_b - best), 0.0)
            total = f_a * s_a[2 + h : 3 + h, :] + f_b * s_b[2 + h : 3 + h, :]
            parts.append(
                (f_a * o_a[head, :].astype(F32) + f_b * o_b[head, :].astype(F32)) / total
            )
        return jnp.concatenate(parts, axis=0).T

    arrive(*send_o1)
    arrive(*send_o2)
    mine = merged(o1s, s1s, o2r.at[0], s2r.at[0])
    other = merged(o1r, s1r, o2r.at[1], s2r.at[1])
    a3[x, :, 0:HW] = jnp.where(yh == 0, mine, other).astype(BF16)
    a3[x, :, HW:] = jnp.where(yh == 0, other, mine).astype(BF16)
    send_a = [remote(AX + k, a3.at[x], a3.at[x], xpeer(k + 1)) for k in range(3)]
    go(*send_a)

    for k in range(3):
        arrive(w2[k], w3[k])
        xk = lax.rem(x + 3 - k, XN)
        copy = remote(W4 + 1 + k, wof.at[xk, :, core], wof.at[xk, :, core], speer)
        go(copy)
        w4.append(copy)

    arrive(*w4)
    st[...] = x_all[...].astype(F32)
    st[...] += dot(a3[x], wof[x].reshape(2 * HW, D))
    for k in (0, 2, 1):
        arrive(send_a[k])
        xk = lax.rem(x + 3 - k, XN)
        st[...] += dot(a3[xk], wof[xk].reshape(2 * HW, D))

    ready(*ld_gu)
    ready(ld_d)
    for half in range(2):
        rows = slice(half * HALF, (half + 1) * HALF)
        stream = st[rows, :].astype(BF16).astype(F32)
        st[rows, :] = stream
        gate_up = dot(normed(stream).astype(BF16), wguv[...])
        gate = gate_up[:, :FF]
        hid[rows, :] = (gate / (1.0 + jnp.exp(-gate)) * gate_up[:, FF:]).astype(BF16)

    def down(half, dst):
        dst[...] = dot(hid[pl.ds(pl.multiple_of(half * HALF, HALF), HALF), :], wdv[...]).astype(BF16)

    def block(k):
        return pl.ds(pl.multiple_of(lax.rem(x + k, XN) * ROWS, ROWS), ROWS)

    down(yf, far)
    send_f = [remote(RF + k, far.at[block(k + 1)], rf.at[k], xpeer(k + 1)) for k in range(3)]
    go(*send_f)
    down(yh, near)
    send_n = [remote(RN + k, near.at[block(k + 1)], rn.at[k], xpeer(k + 1)) for k in range(3)]
    go(*send_n)
    total = far[block(0), :].astype(F32)
    for k in range(3):
        arrive(send_f[k])
        total = total + rf[k].astype(F32)
    ys[...] = total.astype(BF16)
    send_y = remote(RY, ys, yr, ypeer)
    go(send_y)
    total = near[block(0), :].astype(F32)
    for k in range(3):
        arrive(send_n[k])
        total = total + rn[k].astype(F32)
    total = total + st[own_rows, :]
    arrive(send_y)
    out[...] = (total + yr[...].astype(F32)).astype(BF16)
    for copy in started:
        copy.wait_send()


def shards(
    tokens, variate, time_ids, cache_var, cache_len, linked, cache_kv, var_bias,
    w_qkv, w_out, w_gate_up, w_down,
):
    anyspace = pl.BlockSpec(memory_space=pltpu.HBM)
    smem = pl.BlockSpec(memory_space=pltpu.SMEM)
    vmem = pltpu.VMEM
    scratch = [
        vmem((TOK, D), BF16),
        vmem((D, 3 * HW), BF16),
        vmem((KEYS, 2 * HW), BF16),
        vmem((CACHE, HW), BF16),
        vmem((HW, KEYS), BF16),
        vmem((HW, TOK), BF16),
        vmem((2, 2 * HW, TOK), BF16),
        vmem((HW, TOK), BF16),
        vmem((2, 2 * HW, TOK), BF16),
        vmem((2, TOK), jnp.int32),
        vmem((2, TOK), jnp.int32),
        vmem((1, CACHE), jnp.int32),
        vmem((HD // 2, TOK), F32),
        vmem((HD // 2, TOK), F32),
        vmem((HW, TOK), BF16), vmem((8, TOK), F32),
        vmem((HW, TOK), BF16), vmem((8, TOK), F32),
        vmem((HW, TOK), BF16), vmem((8, TOK), F32),
        vmem((2, HW, TOK), BF16), vmem((2, 8, TOK), F32),
        vmem((XN, TOK, 2 * HW), BF16),
        vmem((XN, 2, 2, HD, D), BF16),
        vmem((D, 2 * FF), BF16),
        vmem((FF, D), BF16),
        vmem((TOK, D), F32),
        vmem((TOK, FF), BF16),
        vmem((HALF, D), BF16),
        vmem((HALF, D), BF16),
        vmem((3, ROWS, D), BF16),
        vmem((3, ROWS, D), BF16),
        vmem((ROWS, D), BF16),
        vmem((ROWS, D), BF16),
        pltpu.SemaphoreType.DMA((NSEM,)),
        pltpu.SemaphoreType.DMA((NSEM,)),
        pltpu.SemaphoreType.DMA((14,)),
    ]
    return pl.pallas_call(
        layer,
        out_shape=pltpu.VMEM((ROWS, D), BF16),
        in_specs=[
            anyspace, anyspace, anyspace, anyspace, smem, smem, anyspace, smem,
            anyspace, anyspace, anyspace, anyspace,
        ],
        out_specs=pl.BlockSpec(memory_space=pltpu.VMEM),
        scratch_shapes=scratch,
        compiler_params=pltpu.CompilerParams(
            collective_id=0, has_side_effects=True, vmem_limit_bytes=60 << 20
        ),
        name="layer",
    )(
        tokens, time_ids.reshape(1, TOK), variate.reshape(1, TOK), cache_var.reshape(1, CACHE),
        cache_len, linked, cache_kv, var_bias, w_qkv, w_out, w_gate_up, w_down,
    )


def solution(mesh):
    return jax.shard_map(
        shards,
        mesh=mesh,
        in_specs=(
            P(("group", "tp"), None),
            P("group"),
            P("group"),
            P("group"),
            P("group"),
            P("group"),
            P(None, "group", "tp"),
            P(None, "tp"),
            P(None, None, "tp"),
            P("tp", None),
            P(None, None, "tp"),
            P("tp", None),
        ),
        out_specs=P(("group", "tp"), None),
        check_vma=False,
    )
```

```python
import jax
import jax.numpy as jnp
from jax import lax
from jax.experimental import pallas as pl
from jax.experimental.pallas import tpu as pltpu
from jax.sharding import PartitionSpec as P

F32 = jnp.float32
BF16 = jnp.bfloat16
MASKED = -1e30
GROUPS = 64
TP = 8
XN = 4
ROWS = 32
TOK = 256
HALF = 128
CACHE = 512
KEYS = CACHE + TOK
D = 1024
HW = 128
HD = 64
FF = 512

TC = 2
RC = 2

TY, TX, TF, ME, QQ, O1, O2, AX, W1, W2, W3, W4, RF, RN, RY, NSEM = (
    0, 2, 5, 11, 12, 13, 15, 19, 25, 26, 29, 32, 36, 42, 45, 47,
)


def dot(a, b):
    return jnp.dot(a, b, preferred_element_type=F32)


def normed(values):
    return values * lax.rsqrt(jnp.mean(values * values, axis=-1, keepdims=True) + 1e-05)


def spread(row):
    return jnp.broadcast_to(row, (HW, row.shape[1])).T


def layer(
    tok, tim, var, cvar, clen, lnk, ckv, vb, wqkv, wo, wgu, wd,
    out,
    x_all, wq, ke, vn, vt, qs, qe, qr, qe2, me_s, me_r, cvr, cs, sn,
    o1s, s1s, o1r, s1r, o2s, s2s, o2r, s2r,
    a3, wof, wguv, wdv, st, hid, far, near, rf, rn, ys, yr,
    ssem, rsem, lsem,
):
    g = lax.axis_index("group")
    t = lax.axis_index("tp")
    x = lax.rem(t, XN)
    yh = lax.div(t, XN)
    core = lax.rem(g, 2)
    t_far = lax.rem(t + XN, TP)
    g_par = lax.rem(g + GROUPS // 2, GROUPS)
    g_sib = g + 1 - 2 * core

    def xpeer(k):
        return (g, yh * XN + lax.rem(x + k, XN))

    ypeer = (g, t_far)
    ppeer = (g_par, t)
    fpeer = (g_par, t_far)
    speer = (g_sib, t)

    def remote(slot, src, dst, peer):
        return pltpu.make_async_remote_copy(
            src_ref=src, dst_ref=dst, send_sem=ssem.at[slot], recv_sem=rsem.at[slot],
            device_id=peer, device_id_type=pl.DeviceIdType.MESH,
        )

    loads = []
    loaded = []
    started = []
    arrived = []

    def go(*copies):
        for copy in copies:
            copy.start()
            started.append(copy)

    def arrive(*copies):
        for copy in copies:
            copy.wait_recv()
            arrived.append(copy)

    barrier = pltpu.get_barrier_semaphore()
    for peer in (ypeer, ppeer, fpeer, speer, xpeer(1), xpeer(2), xpeer(3)):
        pl.semaphore_signal(barrier, inc=1, device_id=peer, device_id_type=pl.DeviceIdType.MESH)

    own_rows = pl.ds(pl.multiple_of(t * ROWS, ROWS), ROWS)

    def local(slot, src, dst):
        copy = pltpu.make_async_copy(src, dst, lsem.at[slot])
        copy.start()
        loads.append(copy)
        return copy

    def ready(*copies):
        for copy in copies:
            copy.wait()
            loaded.append(copy)

    ld_tok = local(0, tok, x_all.at[own_rows])
    ld_tim = local(1, tim, me_s.at[pl.ds(0, 1)])
    ld_var = local(2, var, me_s.at[pl.ds(1, 1)])
    ld_cvar = local(3, cvar, cvr)
    ld_w = [local(4 + c, wqkv.at[c], wq.at[:, pl.ds(c * HW, HW)]) for c in range(3)]
    ld_k = local(7, ckv.at[0], ke.at[pl.ds(0, CACHE), pl.ds(0, HW)])
    ld_v = local(8, ckv.at[1], vn)
    ld_wo = [local(9 + c, wo.at[pl.ds(c * HD, HD)], wof.at[x, yh, c]) for c in range(2)]
    ld_gu = [local(11 + c, wgu.at[c], wguv.at[:, pl.ds(c * FF, FF)]) for c in range(2)]
    ld_d = local(13, wd, wdv)
    ready(ld_tim)
    ready(ld_var)

    time_row = me_s[0:1, :].astype(F32)
    var_row = me_s[1:2, :].astype(F32)
    freq = jnp.exp(
        lax.broadcasted_iota(jnp.int32, (HD // 2, TOK), 0).astype(F32) * (-9.210340371976184 / 32)
    )
    angle = freq * time_row
    cs[...] = jnp.cos(angle)
    sn[...] = jnp.sin(angle)

    lane = lax.broadcasted_iota(jnp.int32, (CACHE, HW), 1)
    slot = lax.broadcasted_iota(jnp.int32, (CACHE, HW), 0)
    lane_var = lax.rem(lane, 4).astype(F32)
    in_var = (lane >= HD) & (lane < HD + 12)
    ready(ld_cvar)
    same = jnp.where(spread(cvr[...].astype(F32)) == lane_var, 1.0, 0.0)
    shut = jnp.where(slot >= clen[0], MASKED, 0.0)
    ke[0:CACHE, HW:] = jnp.where(lane < HD, shut, jnp.where(in_var, same, 0.0)).astype(BF16)
    lane = lane[:TOK]
    same = jnp.where(spread(var_row) == lane_var[:TOK], 1.0, 0.0)
    shut = jnp.where(spread(time_row) > lane.astype(F32), MASKED, 0.0)
    ke[CACHE:, HW:] = jnp.where(lane < HD, shut, jnp.where(in_var[:TOK], same, 0.0)).astype(BF16)

    def query_side(dst, times, variates):
        row = lax.broadcasted_iota(jnp.int32, (HD, TOK), 0)
        at_time = jnp.where(row.astype(F32) == times, 1.0, 0.0).astype(BF16)
        hit = lax.rem(row, 4).astype(F32) == variates
        for h in range(2):
            bias = jnp.where(hit, vb[0, h], vb[1, h])
            high = bias.astype(BF16).astype(F32)
            mid = (bias - high).astype(BF16).astype(F32)
            low = bias - high - mid
            parts = jnp.where(
                row < 4, high, jnp.where(row < 8, mid, jnp.where(row < 12, low, 0.0))
            )
            dst[h, HW : HW + HD, :] = at_time
            dst[h, HW + HD :, :] = parts.astype(BF16)
            dst[h, (1 - h) * HD : (2 - h) * HD, :] = jnp.zeros((HD, TOK), BF16)

    query_side(qe, time_row, var_row)
    ready(ld_v)
    vt[:, 0:CACHE] = vn[...].astype(F32).T.astype(BF16)
    ready(ld_tok)
    pl.semaphore_wait(barrier, 7)

    def piece(device, c):
        rows = ROWS // TC
        return x_all.at[pl.ds(pl.multiple_of(device * ROWS + c * rows, rows), rows)]

    tok_y = [remote(TY + c, piece(t, c), piece(t, c), ypeer) for c in range(TC)]
    go(*tok_y)
    tok_x = [remote(TX + k, x_all.at[own_rows], x_all.at[own_rows], xpeer(k + 1)) for k in range(3)]
    go(*tok_x)
    meta = remote(ME, me_s, me_r, ppeer)
    go(meta)

    ready(*ld_w)
    ready(*ld_wo)


    w1 = remote(W1, wof.at[x, yh, core], wof.at[x, yh, core], ypeer)
    go(w1)
    def qkv(half):
        base = pl.multiple_of(half * HALF, HALF)
        rows = pl.ds(base, HALF)
        normal = normed(x_all[rows, :].astype(F32)).astype(BF16)
        prod = dot(normal, wq[...])
        cosine = cs[:, rows]
        sine = sn[:, rows]

        def turned(u):
            parts = []
            for h in range(2):
                lo = u[h * HD : h * HD + HD // 2]
                hi = u[h * HD + HD // 2 : (h + 1) * HD]
                parts += [lo * cosine - hi * sine, hi * cosine + lo * sine]
            return jnp.concatenate(parts, axis=0)

        q = turned(prod[:, 0:HW].T).astype(BF16).astype(F32) * 0.125
        qs[:, rows] = q.astype(BF16)
        k = turned(prod[:, HW : 2 * HW].T)
        v = prod[:, 2 * HW :].T
        new = pl.ds(pl.multiple_of(base + CACHE, HALF), HALF)
        return (new, k, v)

    def keep(new, k, v):
        ke[new, 0:HW] = k.T.astype(BF16)
        vt[:, new] = v.astype(BF16)

    tok_f = []
    for c in range(TC):
        arrive(tok_y[c])
        for k in range(3):
            tok_f.append(
                remote(TF + 3 * c + k, piece(t_far, c), piece(t_far, c), xpeer(k + 1))
            )
            go(tok_f[-1])
    arrive(*tok_x)
    keep(*qkv(yh))
    w2 = [remote(W2 + k, wof.at[x, yh, core], wof.at[x, yh, core], xpeer(k + 1)) for k in range(3)]
    go(*w2)
    arrive(*tok_f)
    rest = qkv(1 - yh)
    send_q = remote(QQ, qs, qr, ppeer)
    go(send_q)
    keep(*rest)
    ready(ld_k)

    def attend(dst, h):
        s = dot(ke[...], dst[h])
        best = jnp.max(s, axis=0, keepdims=True)
        p = jnp.exp(s - best)
        total = jnp.sum(p, axis=0, keepdims=True)
        o = dot(vt[h * HD : (h + 1) * HD, :], p.astype(BF16))
        return o, best, total

    def both_heads(dst, q, o_ref, s_ref):
        s_ref[...] = jnp.zeros(s_ref.shape, F32)
        for h in range(2):
            dst[h, h * HD : (h + 1) * HD, :] = q[h * HD : (h + 1) * HD, :]
            o, best, total = attend(dst, h)
            o_ref[h * HD : (h + 1) * HD, :] = o.astype(BF16)
            s_ref[h : h + 1, :] = best
            s_ref[2 + h : 3 + h, :] = total

    both_heads(qe, qs, o1s, s1s)
    send_o1 = [remote(O1, o1s, o1r, ypeer), remote(O1 + 1, s1s, s1r, ypeer)]
    go(*send_o1)

    yf = 1 - yh
    arrive(w1)
    w3 = [remote(W3 + k, wof.at[x, yf, core], wof.at[x, yf, core], xpeer(k + 1)) for k in range(3)]
    go(*w3)
    w4 = [remote(W4, wof.at[x, yf, core], wof.at[x, yf, core], speer)]
    go(w4[0])
    arrive(meta)
    query_side(qe2, me_r[0:1, :].astype(F32), me_r[1:2, :].astype(F32))
    arrive(send_q)
    both_heads(qe2, qr, o2s, s2s)
    send_o2 = [
        remote(O2, o2s, o2r.at[0], ppeer), remote(O2 + 1, s2s, s2r.at[0], ppeer),
        remote(O2 + 2, o2s, o2r.at[1], fpeer), remote(O2 + 3, s2s, s2r.at[1], fpeer),
    ]
    go(*send_o2)


    def merged(o_a, s_a, o_b, s_b):
        on = lnk[0] > 0
        parts = []
        for h in range(2):
            head = slice(h * HD, (h + 1) * HD)
            m_a = s_a[h : h + 1, :]
            m_b = jnp.where(on, s_b[h : h + 1, :], MASKED)
            best = jnp.maximum(m_a, m_b)
            f_a = jnp.exp(m_a - best)
            f_b = jnp.where(on, jnp.exp(m_b - best), 0.0)
            total = f_a * s_a[2 + h : 3 + h, :] + f_b * s_b[2 + h : 3 + h, :]
            parts.append(
                (f_a * o_a[head, :].astype(F32) + f_b * o_b[head, :].astype(F32)) / total
            )
        return jnp.concatenate(parts, axis=0).T

    send_a = []

    def share(c, upper, heads):
        a3[x, upper] = heads.astype(BF16)
        for k in range(3):
            send_a.append(
                remote(AX + 3 * c + k, a3.at[x, upper], a3.at[x, upper], xpeer(k + 1))
            )
            go(send_a[-1])

    arrive(*send_o2[:2])
    share(0, yh, merged(o1s, s1s, o2r.at[0], s2r.at[0]))
    arrive(*send_o1)
    arrive(*send_o2[2:])
    share(1, yf, merged(o1r, s1r, o2r.at[1], s2r.at[1]))

    for k in range(3):
        arrive(w2[k], w3[k])
        xk = lax.rem(x + 3 - k, XN)
        copy = remote(W4 + 1 + k, wof.at[xk, :, core], wof.at[xk, :, core], speer)
        go(copy)
        w4.append(copy)

    arrive(*w4)
    def out_part(xk):
        heads = jnp.concatenate([a3[xk, 0], a3[xk, 1]], axis=1)
        return dot(heads, wof[xk].reshape(2 * HW, D))

    st[...] = x_all[...].astype(F32)
    st[...] += out_part(x)
    for k in (0, 2, 1):
        arrive(send_a[k], send_a[3 + k])
        xk = lax.rem(x + 3 - k, XN)
        st[...] += out_part(xk)

    ready(*ld_gu)
    ready(ld_d)
    for half in range(2):
        rows = slice(half * HALF, (half + 1) * HALF)
        stream = st[rows, :].astype(BF16).astype(F32)
        st[rows, :] = stream
        gate_up = dot(normed(stream).astype(BF16), wguv[...])
        gate = gate_up[:, :FF]
        hid[rows, :] = (gate / (1.0 + jnp.exp(-gate)) * gate_up[:, FF:]).astype(BF16)

    def down(half, cols):
        rows = pl.ds(pl.multiple_of(half * HALF, HALF), HALF)
        return dot(hid[rows, :], wdv[:, cols]).astype(BF16)

    def block(k):
        return pl.ds(pl.multiple_of(lax.rem(x + k, XN) * ROWS, ROWS), ROWS)

    pieces = [slice(c * (D // RC), (c + 1) * (D // RC)) for c in range(RC)]
    send_f = []
    for c, cols in enumerate(pieces):
        far[c] = down(yf, cols)
        for k in range(3):
            send_f.append(
                remote(RF + 3 * c + k, far.at[c, block(k + 1)], rf.at[c, k], xpeer(k + 1))
            )
            go(send_f[-1])
    near[...] = down(yh, slice(0, D))
    send_n = [remote(RN + k, near.at[block(k + 1)], rn.at[k], xpeer(k + 1)) for k in range(3)]
    go(*send_n)
    send_y = []
    for c in range(RC):
        total = far[c, block(0), :].astype(F32)
        for k in range(3):
            arrive(send_f[3 * c + k])
            total = total + rf[c, k].astype(F32)
        ys[c] = total.astype(BF16)
        send_y.append(remote(RY + c, ys.at[c], yr.at[c], ypeer))
        go(send_y[c])
    total = near[block(0), :].astype(F32)
    for k in range(3):
        arrive(send_n[k])
        total = total + rn[k].astype(F32)
    total = total + st[own_rows, :]
    for c, cols in enumerate(pieces):
        arrive(send_y[c])
        out[:, cols] = (total[:, cols] + yr[c].astype(F32)).astype(BF16)
    for copy in started:
        copy.wait_send()


def shards(
    tokens, variate, time_ids, cache_var, cache_len, linked, cache_kv, var_bias,
    w_qkv, w_out, w_gate_up, w_down,
):
    anyspace = pl.BlockSpec(memory_space=pltpu.HBM)
    smem = pl.BlockSpec(memory_space=pltpu.SMEM)
    vmem = pltpu.VMEM
    scratch = [
        vmem((TOK, D), BF16),
        vmem((D, 3 * HW), BF16),
        vmem((KEYS, 2 * HW), BF16),
        vmem((CACHE, HW), BF16),
        vmem((HW, KEYS), BF16),
        vmem((HW, TOK), BF16),
        vmem((2, 2 * HW, TOK), BF16),
        vmem((HW, TOK), BF16),
        vmem((2, 2 * HW, TOK), BF16),
        vmem((2, TOK), jnp.int32),
        vmem((2, TOK), jnp.int32),
        vmem((1, CACHE), jnp.int32),
        vmem((HD // 2, TOK), F32),
        vmem((HD // 2, TOK), F32),
        vmem((HW, TOK), BF16), vmem((8, TOK), F32),
        vmem((HW, TOK), BF16), vmem((8, TOK), F32),
        vmem((HW, TOK), BF16), vmem((8, TOK), F32),
        vmem((2, HW, TOK), BF16), vmem((2, 8, TOK), F32),
        vmem((XN, 2, TOK, HW), BF16),
        vmem((XN, 2, 2, HD, D), BF16),
        vmem((D, 2 * FF), BF16),
        vmem((FF, D), BF16),
        vmem((TOK, D), F32),
        vmem((TOK, FF), BF16),
        vmem((RC, HALF, D // RC), BF16),
        vmem((HALF, D), BF16),
        vmem((RC, 3, ROWS, D // RC), BF16),
        vmem((3, ROWS, D), BF16),
        vmem((RC, ROWS, D // RC), BF16),
        vmem((RC, ROWS, D // RC), BF16),
        pltpu.SemaphoreType.DMA((NSEM,)),
        pltpu.SemaphoreType.DMA((NSEM,)),
        pltpu.SemaphoreType.DMA((14,)),
    ]
    return pl.pallas_call(
        layer,
        out_shape=pltpu.VMEM((ROWS, D), BF16),
        in_specs=[
            anyspace, anyspace, anyspace, anyspace, smem, smem, anyspace, smem,
            anyspace, anyspace, anyspace, anyspace,
        ],
        out_specs=pl.BlockSpec(memory_space=pltpu.VMEM),
        scratch_shapes=scratch,
        compiler_params=pltpu.CompilerParams(
            collective_id=0, has_side_effects=True, vmem_limit_bytes=60 << 20
        ),
        name="layer",
    )(
        tokens, time_ids.reshape(1, TOK), variate.reshape(1, TOK), cache_var.reshape(1, CACHE),
        cache_len, linked, cache_kv, var_bias, w_qkv, w_out, w_gate_up, w_down,
    )


def solution(mesh):
    return jax.shard_map(
        shards,
        mesh=mesh,
        in_specs=(
            P(("group", "tp"), None),
            P("group"),
            P("group"),
            P("group"),
            P("group"),
            P("group"),
            P(None, "group", "tp"),
            P(None, "tp"),
            P(None, None, "tp"),
            P("tp", None),
            P(None, None, "tp"),
            P("tp", None),
        ),
        out_specs=P(("group", "tp"), None),
        check_vma=False,
    )
```

```python
import jax
import jax.numpy as jnp
from jax import lax
from jax.experimental import pallas as pl
from jax.experimental.pallas import tpu as pltpu
from jax.sharding import PartitionSpec as P

F32 = jnp.float32
BF16 = jnp.bfloat16
MASKED = -1e30
GROUPS = 64
TP = 8
XN = 4
ROWS = 32
TOK = 256
HALF = 128
CACHE = 512
KEYS = CACHE + TOK
D = 1024
HW = 128
HD = 64
FF = 512

TC = 2
RC = 2

TY, TX, TF, ME, QQ, O1, O2, AX, W1, W2, W3, W4, RF, RN, RY, NSEM = (
    0, 2, 5, 11, 12, 14, 17, 23, 29, 30, 33, 36, 40, 46, 49, 51,
)


def dot(a, b):
    return jnp.dot(a, b, preferred_element_type=F32)


def normed(values):
    return values * lax.rsqrt(jnp.mean(values * values, axis=-1, keepdims=True) + 1e-05)


def spread(row):
    return jnp.broadcast_to(row, (HW, row.shape[1])).T


def layer(
    tok, tim, var, cvar, clen, lnk, ckv, vb, wqkv, wo, wgu, wd,
    out,
    x_all, wq, ke, vn, vt, qs, qe, qr, qe2, me_s, me_r, cvr, cs, sn,
    o1s, s1s, o1r, s1r, o2s, s2s, o2r, s2r,
    a3, wof, wguv, wdv, st, hid, far, near, rf, rn, ys, yr,
    ssem, rsem, lsem,
):
    g = lax.axis_index("group")
    t = lax.axis_index("tp")
    x = lax.rem(t, XN)
    yh = lax.div(t, XN)
    core = lax.rem(g, 2)
    t_far = lax.rem(t + XN, TP)
    g_par = lax.rem(g + GROUPS // 2, GROUPS)
    g_sib = g + 1 - 2 * core

    def xpeer(k):
        return (g, yh * XN + lax.rem(x + k, XN))

    ypeer = (g, t_far)
    ppeer = (g_par, t)
    fpeer = (g_par, t_far)
    speer = (g_sib, t)

    def remote(slot, src, dst, peer):
        return pltpu.make_async_remote_copy(
            src_ref=src, dst_ref=dst, send_sem=ssem.at[slot], recv_sem=rsem.at[slot],
            device_id=peer, device_id_type=pl.DeviceIdType.MESH,
        )

    loads = []
    loaded = []
    started = []
    arrived = []

    def go(*copies):
        for copy in copies:
            copy.start()
            started.append(copy)

    def arrive(*copies):
        for copy in copies:
            copy.wait_recv()
            arrived.append(copy)

    barrier = pltpu.get_barrier_semaphore()
    for peer in (ypeer, ppeer, fpeer, speer, xpeer(1), xpeer(2), xpeer(3)):
        pl.semaphore_signal(barrier, inc=1, device_id=peer, device_id_type=pl.DeviceIdType.MESH)

    own_rows = pl.ds(pl.multiple_of(t * ROWS, ROWS), ROWS)

    def local(slot, src, dst):
        copy = pltpu.make_async_copy(src, dst, lsem.at[slot])
        copy.start()
        loads.append(copy)
        return copy

    def ready(*copies):
        for copy in copies:
            copy.wait()
            loaded.append(copy)

    ld_tok = local(0, tok, x_all.at[own_rows])
    ld_tim = local(1, tim, me_s.at[pl.ds(0, 1)])
    ld_var = local(2, var, me_s.at[pl.ds(1, 1)])
    ld_cvar = local(3, cvar, cvr)
    ld_w = [local(4 + c, wqkv.at[c], wq.at[:, pl.ds(c * HW, HW)]) for c in range(3)]
    ld_k = local(7, ckv.at[0], ke.at[pl.ds(0, CACHE), pl.ds(0, HW)])
    ld_v = local(8, ckv.at[1], vn)
    ld_wo = [local(9 + c, wo.at[pl.ds(c * HD, HD)], wof.at[x, yh, c]) for c in range(2)]
    ld_gu = [local(11 + c, wgu.at[c], wguv.at[:, pl.ds(c * FF, FF)]) for c in range(2)]
    ld_d = local(13, wd, wdv)
    ready(ld_tim)
    ready(ld_var)

    time_row = me_s[0:1, :].astype(F32)
    var_row = me_s[1:2, :].astype(F32)
    freq = jnp.exp(
        lax.broadcasted_iota(jnp.int32, (HD // 2, TOK), 0).astype(F32) * (-9.210340371976184 / 32)
    )
    angle = freq * time_row
    cs[...] = jnp.cos(angle)
    sn[...] = jnp.sin(angle)

    lane = lax.broadcasted_iota(jnp.int32, (CACHE, HW), 1)
    slot = lax.broadcasted_iota(jnp.int32, (CACHE, HW), 0)
    lane_var = lax.rem(lane, 4).astype(F32)
    in_var = (lane >= HD) & (lane < HD + 12)
    ready(ld_cvar)
    same = jnp.where(spread(cvr[...].astype(F32)) == lane_var, 1.0, 0.0)
    shut = jnp.where(slot >= clen[0], MASKED, 0.0)
    ke[0:CACHE, HW:] = jnp.where(lane < HD, shut, jnp.where(in_var, same, 0.0)).astype(BF16)
    lane = lane[:TOK]
    same = jnp.where(spread(var_row) == lane_var[:TOK], 1.0, 0.0)
    shut = jnp.where(spread(time_row) > lane.astype(F32), MASKED, 0.0)
    ke[CACHE:, HW:] = jnp.where(lane < HD, shut, jnp.where(in_var[:TOK], same, 0.0)).astype(BF16)

    def query_side(dst, times, variates):
        row = lax.broadcasted_iota(jnp.int32, (HD, TOK), 0)
        at_time = jnp.where(row.astype(F32) == times, 1.0, 0.0).astype(BF16)
        hit = lax.rem(row, 4).astype(F32) == variates
        for h in range(2):
            bias = jnp.where(hit, vb[0, h], vb[1, h])
            high = bias.astype(BF16).astype(F32)
            mid = (bias - high).astype(BF16).astype(F32)
            low = bias - high - mid
            parts = jnp.where(
                row < 4, high, jnp.where(row < 8, mid, jnp.where(row < 12, low, 0.0))
            )
            dst[h, HW : HW + HD, :] = at_time
            dst[h, HW + HD :, :] = parts.astype(BF16)
            dst[h, (1 - h) * HD : (2 - h) * HD, :] = jnp.zeros((HD, TOK), BF16)

    query_side(qe, time_row, var_row)
    ready(ld_v)
    vt[:, 0:CACHE] = vn[...].astype(F32).T.astype(BF16)
    ready(ld_tok)
    pl.semaphore_wait(barrier, 7)

    def piece(device, c):
        rows = ROWS // TC
        return x_all.at[pl.ds(pl.multiple_of(device * ROWS + c * rows, rows), rows)]

    tok_y = [remote(TY + c, piece(t, c), piece(t, c), ypeer) for c in range(TC)]
    go(*tok_y)
    tok_x = [remote(TX + k, x_all.at[own_rows], x_all.at[own_rows], xpeer(k + 1)) for k in range(3)]
    go(*tok_x)
    meta = remote(ME, me_s, me_r, ppeer)
    go(meta)

    ready(*ld_w)
    ready(*ld_wo)


    w1 = remote(W1, wof.at[x, yh, core], wof.at[x, yh, core], ypeer)
    go(w1)
    send_q = []

    def qkv(order, half):
        base = pl.multiple_of(half * HALF, HALF)
        rows = pl.ds(base, HALF)
        normal = normed(x_all[rows, :].astype(F32)).astype(BF16)
        prod = dot(normal, wq[...])
        cosine = cs[:, rows]
        sine = sn[:, rows]

        def turned(u):
            parts = []
            for h in range(2):
                lo = u[h * HD : h * HD + HD // 2]
                hi = u[h * HD + HD // 2 : (h + 1) * HD]
                parts += [lo * cosine - hi * sine, hi * cosine + lo * sine]
            return jnp.concatenate(parts, axis=0)

        q = turned(prod[:, 0:HW].T).astype(BF16).astype(F32) * 0.125
        qs[half] = q.astype(BF16)
        send = remote(QQ + order, qs.at[half], qr.at[half], ppeer)
        go(send)
        send_q.append(send)
        k = turned(prod[:, HW : 2 * HW].T)
        v = prod[:, 2 * HW :].T
        new = pl.ds(pl.multiple_of(base + CACHE, HALF), HALF)
        return (new, k, v)

    def keep(new, k, v):
        ke[new, 0:HW] = k.T.astype(BF16)
        vt[:, new] = v.astype(BF16)

    tok_f = []
    for c in range(TC):
        arrive(tok_y[c])
        for k in range(3):
            tok_f.append(
                remote(TF + 3 * c + k, piece(t_far, c), piece(t_far, c), xpeer(k + 1))
            )
            go(tok_f[-1])
    arrive(*tok_x)
    keep(*qkv(0, yh))
    w2 = [remote(W2 + k, wof.at[x, yh, core], wof.at[x, yh, core], xpeer(k + 1)) for k in range(3)]
    go(*w2)
    arrive(*tok_f)
    rest = qkv(1, 1 - yh)
    keep(*rest)
    ready(ld_k)

    def attend(dst, h):
        s = dot(ke[...], dst[h])
        best = jnp.max(s, axis=0, keepdims=True)
        p = jnp.exp(s - best)
        total = jnp.sum(p, axis=0, keepdims=True)
        o = dot(vt[h * HD : (h + 1) * HD, :], p.astype(BF16))
        return o, best, total

    def both_heads(dst, q, o_ref, s_ref, share_out):
        s_ref[...] = jnp.zeros(s_ref.shape, F32)
        for h in range(2):
            head = slice(h * HD, (h + 1) * HD)
            for half in range(2):
                dst[h, head, half * HALF : (half + 1) * HALF] = q[half, head, :]
            o, best, total = attend(dst, h)
            o_ref[h] = o.astype(BF16)
            s_ref[h : h + 1, :] = best
            s_ref[2 + h : 3 + h, :] = total
            share_out(h)

    send_o1 = []
    send_o2 = [[], []]

    def to_ypeer(h):
        send_o1.append(remote(O1 + h, o1s.at[h], o1r.at[h], ypeer))
        if h == 1:
            send_o1.append(remote(O1 + 2, s1s, s1r, ypeer))
        go(*send_o1[h:])

    def to_partners(h):
        for i, peer in enumerate((ppeer, fpeer)):
            new = [remote(O2 + 3 * i + h, o2s.at[h], o2r.at[i, h], peer)]
            if h == 1:
                new.append(remote(O2 + 3 * i + 2, s2s, s2r.at[i], peer))
            go(*new)
            send_o2[i] += new

    both_heads(qe, qs, o1s, s1s, to_ypeer)

    yf = 1 - yh
    arrive(w1)
    w3 = [remote(W3 + k, wof.at[x, yf, core], wof.at[x, yf, core], xpeer(k + 1)) for k in range(3)]
    go(*w3)
    w4 = [remote(W4, wof.at[x, yf, core], wof.at[x, yf, core], speer)]
    go(w4[0])
    arrive(meta)
    query_side(qe2, me_r[0:1, :].astype(F32), me_r[1:2, :].astype(F32))
    arrive(*send_q)
    both_heads(qe2, qr, o2s, s2s, to_partners)

    def merged(o_a, s_a, o_b, s_b):
        on = lnk[0] > 0
        parts = []
        for h in range(2):
            m_a = s_a[h : h + 1, :]
            m_b = jnp.where(on, s_b[h : h + 1, :], MASKED)
            best = jnp.maximum(m_a, m_b)
            f_a = jnp.exp(m_a - best)
            f_b = jnp.where(on, jnp.exp(m_b - best), 0.0)
            total = f_a * s_a[2 + h : 3 + h, :] + f_b * s_b[2 + h : 3 + h, :]
            parts.append(
                (f_a * o_a[h].astype(F32) + f_b * o_b[h].astype(F32)) / total
            )
        return jnp.concatenate(parts, axis=0).T

    send_a = []

    def share(c, upper, heads):
        a3[x, upper] = heads.astype(BF16)
        for k in range(3):
            send_a.append(
                remote(AX + 3 * c + k, a3.at[x, upper], a3.at[x, upper], xpeer(k + 1))
            )
            go(send_a[-1])

    arrive(*send_o2[0])
    share(0, yh, merged(o1s, s1s, o2r.at[0], s2r.at[0]))
    arrive(*send_o1)
    arrive(*send_o2[1])
    share(1, yf, merged(o1r, s1r, o2r.at[1], s2r.at[1]))

    for k in range(3):
        arrive(w2[k], w3[k])
        xk = lax.rem(x + 3 - k, XN)
        copy = remote(W4 + 1 + k, wof.at[xk, :, core], wof.at[xk, :, core], speer)
        go(copy)
        w4.append(copy)

    arrive(*w4)
    def out_part(xk):
        heads = jnp.concatenate([a3[xk, 0], a3[xk, 1]], axis=1)
        return dot(heads, wof[xk].reshape(2 * HW, D))

    st[...] = x_all[...].astype(F32)
    st[...] += out_part(x)
    for k in (0, 2, 1):
        arrive(send_a[k], send_a[3 + k])
        xk = lax.rem(x + 3 - k, XN)
        st[...] += out_part(xk)

    ready(*ld_gu)
    ready(ld_d)
    for half in range(2):
        rows = slice(half * HALF, (half + 1) * HALF)
        stream = st[rows, :].astype(BF16).astype(F32)
        st[rows, :] = stream
        gate_up = dot(normed(stream).astype(BF16), wguv[...])
        gate = gate_up[:, :FF]
        hid[rows, :] = (gate / (1.0 + jnp.exp(-gate)) * gate_up[:, FF:]).astype(BF16)

    def down(half, cols):
        rows = pl.ds(pl.multiple_of(half * HALF, HALF), HALF)
        return dot(hid[rows, :], wdv[:, cols]).astype(BF16)

    def block(k):
        return pl.ds(pl.multiple_of(lax.rem(x + k, XN) * ROWS, ROWS), ROWS)

    pieces = [slice(c * (D // RC), (c + 1) * (D // RC)) for c in range(RC)]
    send_f = []
    for c, cols in enumerate(pieces):
        far[c] = down(yf, cols)
        for k in range(3):
            send_f.append(
                remote(RF + 3 * c + k, far.at[c, block(k + 1)], rf.at[c, k], xpeer(k + 1))
            )
            go(send_f[-1])
    near[...] = down(yh, slice(0, D))
    send_n = [remote(RN + k, near.at[block(k + 1)], rn.at[k], xpeer(k + 1)) for k in range(3)]
    go(*send_n)
    send_y = []
    for c in range(RC):
        total = far[c, block(0), :].astype(F32)
        for k in range(3):
            arrive(send_f[3 * c + k])
            total = total + rf[c, k].astype(F32)
        ys[c] = total.astype(BF16)
        send_y.append(remote(RY + c, ys.at[c], yr.at[c], ypeer))
        go(send_y[c])
    total = near[block(0), :].astype(F32)
    for k in range(3):
        arrive(send_n[k])
        total = total + rn[k].astype(F32)
    total = total + st[own_rows, :]
    for c, cols in enumerate(pieces):
        arrive(send_y[c])
        out[:, cols] = (total[:, cols] + yr[c].astype(F32)).astype(BF16)
    for copy in started:
        copy.wait_send()


def shards(
    tokens, variate, time_ids, cache_var, cache_len, linked, cache_kv, var_bias,
    w_qkv, w_out, w_gate_up, w_down,
):
    anyspace = pl.BlockSpec(memory_space=pltpu.HBM)
    smem = pl.BlockSpec(memory_space=pltpu.SMEM)
    vmem = pltpu.VMEM
    scratch = [
        vmem((TOK, D), BF16),
        vmem((D, 3 * HW), BF16),
        vmem((KEYS, 2 * HW), BF16),
        vmem((CACHE, HW), BF16),
        vmem((HW, KEYS), BF16),
        vmem((2, HW, HALF), BF16),
        vmem((2, 2 * HW, TOK), BF16),
        vmem((2, HW, HALF), BF16),
        vmem((2, 2 * HW, TOK), BF16),
        vmem((2, TOK), jnp.int32),
        vmem((2, TOK), jnp.int32),
        vmem((1, CACHE), jnp.int32),
        vmem((HD // 2, TOK), F32),
        vmem((HD // 2, TOK), F32),
        vmem((2, HD, TOK), BF16), vmem((8, TOK), F32),
        vmem((2, HD, TOK), BF16), vmem((8, TOK), F32),
        vmem((2, HD, TOK), BF16), vmem((8, TOK), F32),
        vmem((2, 2, HD, TOK), BF16), vmem((2, 8, TOK), F32),
        vmem((XN, 2, TOK, HW), BF16),
        vmem((XN, 2, 2, HD, D), BF16),
        vmem((D, 2 * FF), BF16),
        vmem((FF, D), BF16),
        vmem((TOK, D), F32),
        vmem((TOK, FF), BF16),
        vmem((RC, HALF, D // RC), BF16),
        vmem((HALF, D), BF16),
        vmem((RC, 3, ROWS, D // RC), BF16),
        vmem((3, ROWS, D), BF16),
        vmem((RC, ROWS, D // RC), BF16),
        vmem((RC, ROWS, D // RC), BF16),
        pltpu.SemaphoreType.DMA((NSEM,)),
        pltpu.SemaphoreType.DMA((NSEM,)),
        pltpu.SemaphoreType.DMA((14,)),
    ]
    return pl.pallas_call(
        layer,
        out_shape=pltpu.VMEM((ROWS, D), BF16),
        in_specs=[
            anyspace, anyspace, anyspace, anyspace, smem, smem, anyspace, smem,
            anyspace, anyspace, anyspace, anyspace,
        ],
        out_specs=pl.BlockSpec(memory_space=pltpu.VMEM),
        scratch_shapes=scratch,
        compiler_params=pltpu.CompilerParams(
            collective_id=0, has_side_effects=True, vmem_limit_bytes=60 << 20
        ),
        name="layer",
    )(
        tokens, time_ids.reshape(1, TOK), variate.reshape(1, TOK), cache_var.reshape(1, CACHE),
        cache_len, linked, cache_kv, var_bias, w_qkv, w_out, w_gate_up, w_down,
    )


def solution(mesh):
    return jax.shard_map(
        shards,
        mesh=mesh,
        in_specs=(
            P(("group", "tp"), None),
            P("group"),
            P("group"),
            P("group"),
            P("group"),
            P("group"),
            P(None, "group", "tp"),
            P(None, "tp"),
            P(None, None, "tp"),
            P("tp", None),
            P(None, None, "tp"),
            P("tp", None),
        ),
        out_specs=P(("group", "tp"), None),
        check_vma=False,
    )
```

```python
import jax
import jax.numpy as jnp
from jax import lax
from jax.experimental import pallas as pl
from jax.experimental.pallas import tpu as pltpu
from jax.sharding import PartitionSpec as P

F32 = jnp.float32
BF16 = jnp.bfloat16
MASKED = -1e30
GROUPS = 64
TP = 8
XN = 4
ROWS = 32
TOK = 256
HALF = 128
CACHE = 512
KEYS = CACHE + TOK
D = 1024
HW = 128
HD = 64
FF = 512

TC = 2
RC = 2

TY, TX, TF, ME, QQ, O1, O2, AX, W1, W2, W3, W4, RF, RN, RY, NSEM = (
    0, 2, 5, 11, 12, 14, 17, 23, 29, 30, 33, 36, 40, 46, 49, 51,
)


def dot(a, b):
    return jnp.dot(a, b, preferred_element_type=F32)


def normed(values):
    return values * lax.rsqrt(jnp.mean(values * values, axis=-1, keepdims=True) + 1e-05)


def spread(row):
    return jnp.broadcast_to(row, (HW, row.shape[1])).T


def layer(
    tok, tim, var, cvar, clen, lnk, ckv, vb, wqkv, wo, wgu, wd,
    out,
    x_all, wq, ke, vn, vt, qs, qe, qr, qe2, me_s, me_r, cvr, cs, sn,
    o1s, s1s, o1r, s1r, o2s, s2s, o2r, s2r,
    a3, wof, wguv, wdv, st, hid, far, near, rf, rn, ys, yr,
    ssem, rsem, lsem,
):
    g = lax.axis_index("group")
    t = lax.axis_index("tp")
    x = lax.rem(t, XN)
    yh = lax.div(t, XN)
    core = lax.rem(g, 2)
    t_far = lax.rem(t + XN, TP)
    g_par = lax.rem(g + GROUPS // 2, GROUPS)
    g_sib = g + 1 - 2 * core

    def xpeer(k):
        return (g, yh * XN + lax.rem(x + k, XN))

    ypeer = (g, t_far)
    ppeer = (g_par, t)
    fpeer = (g_par, t_far)
    speer = (g_sib, t)

    def remote(slot, src, dst, peer):
        return pltpu.make_async_remote_copy(
            src_ref=src, dst_ref=dst, send_sem=ssem.at[slot], recv_sem=rsem.at[slot],
            device_id=peer, device_id_type=pl.DeviceIdType.MESH,
        )

    loads = []
    loaded = []
    started = []
    arrived = []

    def go(*copies):
        for copy in copies:
            copy.start()
            started.append(copy)

    def arrive(*copies):
        for copy in copies:
            copy.wait_recv()
            arrived.append(copy)

    barrier = pltpu.get_barrier_semaphore()
    for peer in (ypeer, ppeer, fpeer, speer, xpeer(1), xpeer(2), xpeer(3)):
        pl.semaphore_signal(barrier, inc=1, device_id=peer, device_id_type=pl.DeviceIdType.MESH)

    own_rows = pl.ds(pl.multiple_of(t * ROWS, ROWS), ROWS)

    def local(slot, src, dst):
        copy = pltpu.make_async_copy(src, dst, lsem.at[slot])
        copy.start()
        loads.append(copy)
        return copy

    def ready(*copies):
        for copy in copies:
            copy.wait()
            loaded.append(copy)

    ld_tok = local(0, tok, x_all.at[own_rows])
    ld_tim = local(1, tim, me_s.at[pl.ds(0, 1)])
    ld_var = local(2, var, me_s.at[pl.ds(1, 1)])
    ld_cvar = local(3, cvar, cvr)
    ld_w = [local(4 + c, wqkv.at[c], wq.at[:, pl.ds(c * HW, HW)]) for c in range(3)]
    ld_k = local(7, ckv.at[0], ke.at[pl.ds(0, CACHE), pl.ds(0, HW)])
    ld_v = local(8, ckv.at[1], vn)
    ld_wo = [local(9 + c, wo.at[pl.ds(c * HD, HD)], wof.at[x, yh, c]) for c in range(2)]
    ld_gu = [local(11 + c, wgu.at[c], wguv.at[:, pl.ds(c * FF, FF)]) for c in range(2)]
    ld_d = local(13, wd, wdv)
    ready(ld_tim)
    ready(ld_var)

    time_row = me_s[0:1, :].astype(F32)
    var_row = me_s[1:2, :].astype(F32)
    freq = jnp.exp(
        lax.broadcasted_iota(jnp.int32, (HD // 2, TOK), 0).astype(F32) * (-9.210340371976184 / 32)
    )
    angle = freq * time_row
    cs[...] = jnp.cos(angle)
    sn[...] = jnp.sin(angle)

    lane = lax.broadcasted_iota(jnp.int32, (CACHE, HW), 1)
    slot = lax.broadcasted_iota(jnp.int32, (CACHE, HW), 0)
    lane_var = lax.rem(lane, 4).astype(F32)
    in_var = (lane >= HD) & (lane < HD + 12)
    ready(ld_cvar)
    same = jnp.where(spread(cvr[...].astype(F32)) == lane_var, 1.0, 0.0)
    shut = jnp.where(slot >= clen[0], MASKED, 0.0)
    ke[0:CACHE, HW:] = jnp.where(lane < HD, shut, jnp.where(in_var, same, 0.0)).astype(BF16)
    lane = lane[:TOK]
    same = jnp.where(spread(var_row) == lane_var[:TOK], 1.0, 0.0)
    shut = jnp.where(spread(time_row) > lane.astype(F32), MASKED, 0.0)
    ke[CACHE:, HW:] = jnp.where(lane < HD, shut, jnp.where(in_var[:TOK], same, 0.0)).astype(BF16)

    def query_side(dst, times, variates):
        row = lax.broadcasted_iota(jnp.int32, (HD, TOK), 0)
        at_time = jnp.where(row.astype(F32) == times, 1.0, 0.0).astype(BF16)
        hit = lax.rem(row, 4).astype(F32) == variates
        for h in range(2):
            bias = jnp.where(hit, vb[0, h], vb[1, h])
            high = bias.astype(BF16).astype(F32)
            mid = (bias - high).astype(BF16).astype(F32)
            low = bias - high - mid
            parts = jnp.where(
                row < 4, high, jnp.where(row < 8, mid, jnp.where(row < 12, low, 0.0))
            )
            dst[h, HW : HW + HD, :] = at_time
            dst[h, HW + HD :, :] = parts.astype(BF16)
            dst[h, (1 - h) * HD : (2 - h) * HD, :] = jnp.zeros((HD, TOK), BF16)

    query_side(qe, time_row, var_row)
    ready(ld_v)
    vt[:, 0:CACHE] = vn[...].astype(F32).T.astype(BF16)
    ready(ld_tok)
    pl.semaphore_wait(barrier, 7)

    def piece(device, c):
        rows = ROWS // TC
        return x_all.at[pl.ds(pl.multiple_of(device * ROWS + c * rows, rows), rows)]

    tok_y = [remote(TY + c, piece(t, c), piece(t, c), ypeer) for c in range(TC)]
    go(*tok_y)
    tok_x = [remote(TX + k, x_all.at[own_rows], x_all.at[own_rows], xpeer(k + 1)) for k in range(3)]
    go(*tok_x)
    meta = remote(ME, me_s, me_r, ppeer)
    go(meta)

    ready(*ld_w)
    ready(*ld_wo)


    w1 = remote(W1, wof.at[x, yh, core], wof.at[x, yh, core], ypeer)
    go(w1)
    send_q = []

    def qkv(order, half):
        base = pl.multiple_of(half * HALF, HALF)
        rows = pl.ds(base, HALF)
        normal = normed(x_all[rows, :].astype(F32)).astype(BF16)
        prod = dot(normal, wq[...])
        cosine = cs[:, rows]
        sine = sn[:, rows]

        def turned(u):
            parts = []
            for h in range(2):
                lo = u[h * HD : h * HD + HD // 2]
                hi = u[h * HD + HD // 2 : (h + 1) * HD]
                parts += [lo * cosine - hi * sine, hi * cosine + lo * sine]
            return jnp.concatenate(parts, axis=0)

        q = turned(prod[:, 0:HW].T).astype(BF16).astype(F32) * 0.125
        qs[half] = q.astype(BF16)
        send = remote(QQ + order, qs.at[half], qr.at[half], ppeer)
        go(send)
        send_q.append(send)
        k = turned(prod[:, HW : 2 * HW].T)
        v = prod[:, 2 * HW :].T
        new = pl.ds(pl.multiple_of(base + CACHE, HALF), HALF)
        return (new, k, v)

    def keep(new, k, v):
        ke[new, 0:HW] = k.T.astype(BF16)
        vt[:, new] = v.astype(BF16)

    tok_f = []
    for c in range(TC):
        arrive(tok_y[c])
        for k in range(3):
            tok_f.append(
                remote(TF + 3 * c + k, piece(t_far, c), piece(t_far, c), xpeer(k + 1))
            )
            go(tok_f[-1])
    arrive(*tok_x)
    keep(*qkv(0, yh))
    w2 = [remote(W2 + k, wof.at[x, yh, core], wof.at[x, yh, core], xpeer(k + 1)) for k in range(3)]
    go(*w2)
    arrive(*tok_f)
    rest = qkv(1, 1 - yh)
    keep(*rest)
    ready(ld_k)

    def attend(dst, h):
        s = dot(ke[...], dst[h])
        best = jnp.max(s, axis=0, keepdims=True)
        p = jnp.exp(s - best)
        total = jnp.sum(p, axis=0, keepdims=True)
        o = dot(vt[h * HD : (h + 1) * HD, :], p.astype(BF16))
        return o, best, total

    def both_heads(dst, q, o_ref, s_ref, share_out):
        s_ref[...] = jnp.zeros(s_ref.shape, F32)
        for h in range(2):
            head = slice(h * HD, (h + 1) * HD)
            for half in range(2):
                dst[h, head, half * HALF : (half + 1) * HALF] = q[half, head, :]
            o, best, total = attend(dst, h)
            o_ref[h] = o.astype(BF16)
            s_ref[h : h + 1, :] = best
            s_ref[2 + h : 3 + h, :] = total
            share_out(h)

    send_o1 = []
    send_o2 = [[], []]

    def to_ypeer(h):
        send_o1.append(remote(O1 + h, o1s.at[h], o1r.at[h], ypeer))
        if h == 1:
            send_o1.append(remote(O1 + 2, s1s, s1r, ypeer))
        go(*send_o1[h:])

    def to_partners(h):
        for i, peer in enumerate((ppeer, fpeer)):
            new = [remote(O2 + 3 * i + h, o2s.at[h], o2r.at[i, h], peer)]
            if h == 1:
                new.append(remote(O2 + 3 * i + 2, s2s, s2r.at[i], peer))
            go(*new)
            send_o2[i] += new

    both_heads(qe, qs, o1s, s1s, to_ypeer)

    yf = 1 - yh
    arrive(w1)
    w3 = [remote(W3 + k, wof.at[x, yf, core], wof.at[x, yf, core], xpeer(k + 1)) for k in range(3)]
    go(*w3)
    w4 = [remote(W4, wof.at[x, yf, core], wof.at[x, yf, core], speer)]
    go(w4[0])
    arrive(meta)
    query_side(qe2, me_r[0:1, :].astype(F32), me_r[1:2, :].astype(F32))
    arrive(*send_q)
    both_heads(qe2, qr, o2s, s2s, to_partners)

    def merged(o_a, s_a, o_b, s_b):
        on = lnk[0] > 0
        parts = []
        for h in range(2):
            m_a = s_a[h : h + 1, :]
            m_b = jnp.where(on, s_b[h : h + 1, :], MASKED)
            best = jnp.maximum(m_a, m_b)
            f_a = jnp.exp(m_a - best)
            f_b = jnp.where(on, jnp.exp(m_b - best), 0.0)
            total = f_a * s_a[2 + h : 3 + h, :] + f_b * s_b[2 + h : 3 + h, :]
            parts.append(
                (f_a * o_a[h].astype(F32) + f_b * o_b[h].astype(F32)) / total
            )
        return jnp.concatenate(parts, axis=0).T

    send_a = []

    def share(c, upper, heads):
        a3[x, upper] = heads.astype(BF16)
        for k in range(3):
            send_a.append(
                remote(AX + 3 * c + k, a3.at[x, upper], a3.at[x, upper], xpeer(k + 1))
            )
            go(send_a[-1])

    arrive(*send_o2[0])
    share(0, yh, merged(o1s, s1s, o2r.at[0], s2r.at[0]))
    arrive(*send_o1)
    arrive(*send_o2[1])
    share(1, yf, merged(o1r, s1r, o2r.at[1], s2r.at[1]))

    for k in range(3):
        arrive(w2[k], w3[k])
        xk = lax.rem(x + 3 - k, XN)
        copy = remote(W4 + 1 + k, wof.at[xk, :, core], wof.at[xk, :, core], speer)
        go(copy)
        w4.append(copy)

    def half_rows(half):
        return pl.ds(pl.multiple_of(half * HALF, HALF), HALF)

    def out_part(rows, xk):
        heads = jnp.concatenate([a3[xk, 0, rows, :], a3[xk, 1, rows, :]], axis=1)
        st[rows, :] += dot(heads, wof[xk].reshape(2 * HW, D))

    def feed(half, first):
        rows = half_rows(half)
        st[rows, :] = x_all[rows, :].astype(F32)
        if first:
            arrive(w4[0])
        out_part(rows, x)
        for k in (0, 2, 1):
            if first:
                arrive(w4[1 + k], send_a[k], send_a[3 + k])
            out_part(rows, lax.rem(x + 3 - k, XN))
        if first:
            ready(*ld_gu)
            ready(ld_d)
        stream = st[rows, :].astype(BF16).astype(F32)
        st[rows, :] = stream
        gate_up = dot(normed(stream).astype(BF16), wguv[...])
        gate = gate_up[:, :FF]
        hid[rows, :] = (gate / (1.0 + jnp.exp(-gate)) * gate_up[:, FF:]).astype(BF16)

    feed(yf, True)
    def down(half, cols):
        return dot(hid[half_rows(half), :], wdv[:, cols]).astype(BF16)

    def block(k):
        return pl.ds(pl.multiple_of(lax.rem(x + k, XN) * ROWS, ROWS), ROWS)

    pieces = [slice(c * (D // RC), (c + 1) * (D // RC)) for c in range(RC)]
    send_f = []
    for c, cols in enumerate(pieces):
        far[c] = down(yf, cols)
        for k in range(3):
            send_f.append(
                remote(RF + 3 * c + k, far.at[c, block(k + 1)], rf.at[c, k], xpeer(k + 1))
            )
            go(send_f[-1])
    feed(yh, False)
    near[...] = down(yh, slice(0, D))
    send_n = [remote(RN + k, near.at[block(k + 1)], rn.at[k], xpeer(k + 1)) for k in range(3)]
    go(*send_n)
    send_y = []
    for c in range(RC):
        total = far[c, block(0), :].astype(F32)
        for k in range(3):
            arrive(send_f[3 * c + k])
            total = total + rf[c, k].astype(F32)
        ys[c] = total.astype(BF16)
        send_y.append(remote(RY + c, ys.at[c], yr.at[c], ypeer))
        go(send_y[c])
    total = near[block(0), :].astype(F32)
    for k in range(3):
        arrive(send_n[k])
        total = total + rn[k].astype(F32)
    total = total + st[own_rows, :]
    for c, cols in enumerate(pieces):
        arrive(send_y[c])
        out[:, cols] = (total[:, cols] + yr[c].astype(F32)).astype(BF16)
    for copy in started:
        copy.wait_send()


def shards(
    tokens, variate, time_ids, cache_var, cache_len, linked, cache_kv, var_bias,
    w_qkv, w_out, w_gate_up, w_down,
):
    anyspace = pl.BlockSpec(memory_space=pltpu.HBM)
    smem = pl.BlockSpec(memory_space=pltpu.SMEM)
    vmem = pltpu.VMEM
    scratch = [
        vmem((TOK, D), BF16),
        vmem((D, 3 * HW), BF16),
        vmem((KEYS, 2 * HW), BF16),
        vmem((CACHE, HW), BF16),
        vmem((HW, KEYS), BF16),
        vmem((2, HW, HALF), BF16),
        vmem((2, 2 * HW, TOK), BF16),
        vmem((2, HW, HALF), BF16),
        vmem((2, 2 * HW, TOK), BF16),
        vmem((2, TOK), jnp.int32),
        vmem((2, TOK), jnp.int32),
        vmem((1, CACHE), jnp.int32),
        vmem((HD // 2, TOK), F32),
        vmem((HD // 2, TOK), F32),
        vmem((2, HD, TOK), BF16), vmem((8, TOK), F32),
        vmem((2, HD, TOK), BF16), vmem((8, TOK), F32),
        vmem((2, HD, TOK), BF16), vmem((8, TOK), F32),
        vmem((2, 2, HD, TOK), BF16), vmem((2, 8, TOK), F32),
        vmem((XN, 2, TOK, HW), BF16),
        vmem((XN, 2, 2, HD, D), BF16),
        vmem((D, 2 * FF), BF16),
        vmem((FF, D), BF16),
        vmem((TOK, D), F32),
        vmem((TOK, FF), BF16),
        vmem((RC, HALF, D // RC), BF16),
        vmem((HALF, D), BF16),
        vmem((RC, 3, ROWS, D // RC), BF16),
        vmem((3, ROWS, D), BF16),
        vmem((RC, ROWS, D // RC), BF16),
        vmem((RC, ROWS, D // RC), BF16),
        pltpu.SemaphoreType.DMA((NSEM,)),
        pltpu.SemaphoreType.DMA((NSEM,)),
        pltpu.SemaphoreType.DMA((14,)),
    ]
    return pl.pallas_call(
        layer,
        out_shape=pltpu.VMEM((ROWS, D), BF16),
        in_specs=[
            anyspace, anyspace, anyspace, anyspace, smem, smem, anyspace, smem,
            anyspace, anyspace, anyspace, anyspace,
        ],
        out_specs=pl.BlockSpec(memory_space=pltpu.VMEM),
        scratch_shapes=scratch,
        compiler_params=pltpu.CompilerParams(
            collective_id=0, has_side_effects=True, vmem_limit_bytes=60 << 20
        ),
        name="layer",
    )(
        tokens, time_ids.reshape(1, TOK), variate.reshape(1, TOK), cache_var.reshape(1, CACHE),
        cache_len, linked, cache_kv, var_bias, w_qkv, w_out, w_gate_up, w_down,
    )


def solution(mesh):
    return jax.shard_map(
        shards,
        mesh=mesh,
        in_specs=(
            P(("group", "tp"), None),
            P("group"),
            P("group"),
            P("group"),
            P("group"),
            P("group"),
            P(None, "group", "tp"),
            P(None, "tp"),
            P(None, None, "tp"),
            P("tp", None),
            P(None, None, "tp"),
            P("tp", None),
        ),
        out_specs=P(("group", "tp"), None),
        check_vma=False,
    )
```

```python
import jax
import jax.numpy as jnp
from jax import lax
from jax.experimental import pallas as pl
from jax.experimental.pallas import tpu as pltpu
from jax.sharding import PartitionSpec as P

F32 = jnp.float32
BF16 = jnp.bfloat16
MASKED = -1e30
GROUPS = 64
TP = 8
XN = 4
ROWS = 32
TOK = 256
HALF = 128
CACHE = 512
KEYS = CACHE + TOK
D = 1024
HW = 128
HD = 64
FF = 512

TC = 2
RC = 2

TY, TX, TF, ME, QQ, O1, O2, AX, W1, W2, W3, W4, RF, RN, RY, NSEM = (
    0, 2, 5, 11, 12, 14, 17, 23, 29, 30, 33, 36, 40, 46, 49, 51,
)


def dot(a, b):
    return jnp.dot(a, b, preferred_element_type=F32)


def normed(values):
    return values * lax.rsqrt(jnp.mean(values * values, axis=-1, keepdims=True) + 1e-05)


def spread(row):
    return jnp.broadcast_to(row, (HW, row.shape[1])).T


def layer(
    tok, tim, var, cvar, clen, lnk, ckv, vb, wqkv, wo, wgu, wd,
    out,
    x_all, wq, ke, vn, vt, qs, qe, qr, qe2, me_s, me_r, cvr, cs, sn,
    o1s, s1s, o1r, s1r, o2s, s2s, o2r, s2r,
    a3, wof, wguv, wdv, st, hid, far, near, rf, rn, ys, yr,
    ssem, rsem, lsem,
):
    g = lax.axis_index("group")
    t = lax.axis_index("tp")
    x = lax.rem(t, XN)
    yh = lax.div(t, XN)
    core = lax.rem(g, 2)
    t_far = lax.rem(t + XN, TP)
    g_par = lax.rem(g + GROUPS // 2, GROUPS)
    g_sib = g + 1 - 2 * core

    def xpeer(k):
        return (g, yh * XN + lax.rem(x + k, XN))

    ypeer = (g, t_far)
    ppeer = (g_par, t)
    fpeer = (g_par, t_far)
    speer = (g_sib, t)

    def remote(slot, src, dst, peer):
        return pltpu.make_async_remote_copy(
            src_ref=src, dst_ref=dst, send_sem=ssem.at[slot], recv_sem=rsem.at[slot],
            device_id=peer, device_id_type=pl.DeviceIdType.MESH,
        )

    loads = []
    loaded = []
    started = []
    arrived = []

    def go(*copies):
        for copy in copies:
            copy.start()
            started.append(copy)

    def arrive(*copies):
        for copy in copies:
            copy.wait_recv()
            arrived.append(copy)

    barrier = pltpu.get_barrier_semaphore()
    for peer in (ypeer, ppeer, fpeer, speer, xpeer(1), xpeer(2), xpeer(3)):
        pl.semaphore_signal(barrier, inc=1, device_id=peer, device_id_type=pl.DeviceIdType.MESH)

    own_rows = pl.ds(pl.multiple_of(t * ROWS, ROWS), ROWS)

    def local(slot, src, dst):
        copy = pltpu.make_async_copy(src, dst, lsem.at[slot])
        copy.start()
        loads.append(copy)
        return copy

    def ready(*copies):
        for copy in copies:
            copy.wait()
            loaded.append(copy)

    ld_tok = local(0, tok, x_all.at[own_rows])
    ld_tim = local(1, tim, me_s.at[pl.ds(0, 1)])
    ld_var = local(2, var, me_s.at[pl.ds(1, 1)])
    ld_cvar = local(3, cvar, cvr)
    ld_w = [local(4 + c, wqkv.at[c], wq.at[:, pl.ds(c * HW, HW)]) for c in range(3)]
    ld_k = local(7, ckv.at[0], ke.at[pl.ds(0, CACHE), pl.ds(0, HW)])
    ld_v = local(8, ckv.at[1], vn)
    ld_wo = [local(9 + c, wo.at[pl.ds(c * HD, HD)], wof.at[x, yh, c]) for c in range(2)]
    ld_gu = [local(11 + c, wgu.at[c], wguv.at[:, pl.ds(c * FF, FF)]) for c in range(2)]
    ld_d = local(13, wd, wdv)
    ready(ld_tim)
    ready(ld_var)

    time_row = me_s[0:1, :].astype(F32)
    var_row = me_s[1:2, :].astype(F32)
    freq = jnp.exp(
        lax.broadcasted_iota(jnp.int32, (HD // 2, TOK), 0).astype(F32) * (-9.210340371976184 / 32)
    )
    angle = freq * time_row
    cs[...] = jnp.cos(angle)
    sn[...] = jnp.sin(angle)

    lane = lax.broadcasted_iota(jnp.int32, (CACHE, HW), 1)
    slot = lax.broadcasted_iota(jnp.int32, (CACHE, HW), 0)
    lane_var = lax.rem(lane, 4).astype(F32)
    in_var = (lane >= HD) & (lane < HD + 12)
    ready(ld_cvar)
    same = jnp.where(spread(cvr[...].astype(F32)) == lane_var, 1.0, 0.0)
    shut = jnp.where(slot >= clen[0], MASKED, 0.0)
    ke[0:CACHE, HW:] = jnp.where(lane < HD, shut, jnp.where(in_var, same, 0.0)).astype(BF16)
    lane = lane[:TOK]
    same = jnp.where(spread(var_row) == lane_var[:TOK], 1.0, 0.0)
    shut = jnp.where(spread(time_row) > lane.astype(F32), MASKED, 0.0)
    ke[CACHE:, HW:] = jnp.where(lane < HD, shut, jnp.where(in_var[:TOK], same, 0.0)).astype(BF16)

    def query_side(dst, times, variates):
        row = lax.broadcasted_iota(jnp.int32, (HD, TOK), 0)
        at_time = jnp.where(row.astype(F32) == times, 1.0, 0.0).astype(BF16)
        hit = lax.rem(row, 4).astype(F32) == variates
        for h in range(2):
            bias = jnp.where(hit, vb[0, h], vb[1, h])
            high = bias.astype(BF16).astype(F32)
            mid = (bias - high).astype(BF16).astype(F32)
            low = bias - high - mid
            parts = jnp.where(
                row < 4, high, jnp.where(row < 8, mid, jnp.where(row < 12, low, 0.0))
            )
            dst[h, HW : HW + HD, :] = at_time
            dst[h, HW + HD :, :] = parts.astype(BF16)
            dst[h, (1 - h) * HD : (2 - h) * HD, :] = jnp.zeros((HD, TOK), BF16)

    query_side(qe, time_row, var_row)
    ready(ld_v)
    vt[:, 0:CACHE] = vn[...].astype(F32).T.astype(BF16)
    ready(ld_tok)
    pl.semaphore_wait(barrier, 7)

    def piece(device, c):
        rows = ROWS // TC
        return x_all.at[pl.ds(pl.multiple_of(device * ROWS + c * rows, rows), rows)]

    tok_y = [remote(TY + c, piece(t, c), piece(t, c), ypeer) for c in range(TC)]
    go(*tok_y)
    tok_x = [remote(TX + k, x_all.at[own_rows], x_all.at[own_rows], xpeer(k + 1)) for k in range(3)]
    go(*tok_x)
    meta = remote(ME, me_s, me_r, ppeer)
    go(meta)

    ready(*ld_w)
    ready(*ld_wo)


    w1 = remote(W1, wof.at[x, yh, core], wof.at[x, yh, core], ypeer)
    go(w1)
    send_q = []

    def qkv(order, half):
        base = pl.multiple_of(half * HALF, HALF)
        rows = pl.ds(base, HALF)
        normal = normed(x_all[rows, :].astype(F32)).astype(BF16)
        prod = dot(normal, wq[...])
        cosine = cs[:, rows]
        sine = sn[:, rows]

        def turned(u):
            parts = []
            for h in range(2):
                lo = u[h * HD : h * HD + HD // 2]
                hi = u[h * HD + HD // 2 : (h + 1) * HD]
                parts += [lo * cosine - hi * sine, hi * cosine + lo * sine]
            return jnp.concatenate(parts, axis=0)

        q = turned(prod[:, 0:HW].T).astype(BF16).astype(F32) * 0.125
        qs[half] = q.astype(BF16)
        send = remote(QQ + order, qs.at[half], qr.at[half], ppeer)
        go(send)
        send_q.append(send)
        k = turned(prod[:, HW : 2 * HW].T)
        v = prod[:, 2 * HW :].T
        new = pl.ds(pl.multiple_of(base + CACHE, HALF), HALF)
        return (new, k, v)

    def keep(new, k, v):
        ke[new, 0:HW] = k.T.astype(BF16)
        vt[:, new] = v.astype(BF16)

    tok_f = []
    for c in range(TC):
        arrive(tok_y[c])
        for k in range(3):
            tok_f.append(
                remote(TF + 3 * c + k, piece(t_far, c), piece(t_far, c), xpeer(k + 1))
            )
            go(tok_f[-1])
    arrive(*tok_x)
    keep(*qkv(0, yh))
    w2 = [remote(W2 + k, wof.at[x, yh, core], wof.at[x, yh, core], xpeer(k + 1)) for k in range(3)]
    go(*w2)
    arrive(*tok_f)
    rest = qkv(1, 1 - yh)
    keep(*rest)
    ready(ld_k)

    def attend(dst, h):
        s = dot(ke[...], dst[h])
        best = jnp.max(s, axis=0, keepdims=True)
        p = jnp.exp(s - best)
        total = jnp.sum(p, axis=0, keepdims=True)
        o = dot(vt[h * HD : (h + 1) * HD, :], p.astype(BF16))
        return o, best, total

    def both_heads(dst, q, o_ref, s_ref, share_out):
        s_ref[...] = jnp.zeros(s_ref.shape, F32)
        for h in range(2):
            head = slice(h * HD, (h + 1) * HD)
            for half in range(2):
                dst[h, head, half * HALF : (half + 1) * HALF] = q[half, head, :]
            o, best, total = attend(dst, h)
            o_ref[h] = o.astype(BF16)
            s_ref[h : h + 1, :] = best
            s_ref[2 + h : 3 + h, :] = total
            share_out(h)

    send_o1 = []
    send_o2 = [[], []]

    def to_ypeer(h):
        send_o1.append(remote(O1 + h, o1s.at[h], o1r.at[h], ypeer))
        if h == 1:
            send_o1.append(remote(O1 + 2, s1s, s1r, ypeer))
        go(*send_o1[h:])

    def to_partners(h):
        new = [remote(O2 + h, o2s.at[h], o2r.at[0, h], ppeer)]
        if h == 1:
            new.append(remote(O2 + 2, s2s, s2r.at[0], ppeer))
        go(*new)
        send_o2[0].extend(new)
        if h == 1:
            new = [remote(O2 + 3 + i, o2s.at[i], o2r.at[1, i], fpeer) for i in range(2)]
            new.append(remote(O2 + 5, s2s, s2r.at[1], fpeer))
            go(*new)
            send_o2[1].extend(new)

    both_heads(qe, qs, o1s, s1s, to_ypeer)

    yf = 1 - yh
    arrive(w1)
    w3 = [remote(W3 + k, wof.at[x, yf, core], wof.at[x, yf, core], xpeer(k + 1)) for k in range(3)]
    go(*w3)
    w4 = [remote(W4, wof.at[x, yf, core], wof.at[x, yf, core], speer)]
    go(w4[0])
    arrive(meta)
    query_side(qe2, me_r[0:1, :].astype(F32), me_r[1:2, :].astype(F32))
    arrive(*send_q)
    both_heads(qe2, qr, o2s, s2s, to_partners)

    def merged(o_a, s_a, o_b, s_b):
        on = lnk[0] > 0
        parts = []
        for h in range(2):
            m_a = s_a[h : h + 1, :]
            m_b = jnp.where(on, s_b[h : h + 1, :], MASKED)
            best = jnp.maximum(m_a, m_b)
            f_a = jnp.exp(m_a - best)
            f_b = jnp.where(on, jnp.exp(m_b - best), 0.0)
            total = f_a * s_a[2 + h : 3 + h, :] + f_b * s_b[2 + h : 3 + h, :]
            parts.append(
                (f_a * o_a[h].astype(F32) + f_b * o_b[h].astype(F32)) / total
            )
        return jnp.concatenate(parts, axis=0).T

    send_a = []

    def share(c, upper, heads):
        a3[x, upper] = heads.astype(BF16)
        for k in range(3):
            send_a.append(
                remote(AX + 3 * c + k, a3.at[x, upper], a3.at[x, upper], xpeer(k + 1))
            )
            go(send_a[-1])

    arrive(*send_o2[0])
    share(0, yh, merged(o1s, s1s, o2r.at[0], s2r.at[0]))
    arrive(*send_o1)
    arrive(*send_o2[1])
    share(1, yf, merged(o1r, s1r, o2r.at[1], s2r.at[1]))

    for k in range(3):
        arrive(w2[k], w3[k])
        xk = lax.rem(x + 3 - k, XN)
        copy = remote(W4 + 1 + k, wof.at[xk, :, core], wof.at[xk, :, core], speer)
        go(copy)
        w4.append(copy)

    def half_rows(half):
        return pl.ds(pl.multiple_of(half * HALF, HALF), HALF)

    def out_part(rows, xk):
        heads = jnp.concatenate([a3[xk, 0, rows, :], a3[xk, 1, rows, :]], axis=1)
        st[rows, :] += dot(heads, wof[xk].reshape(2 * HW, D))

    def feed(half, first):
        rows = half_rows(half)
        st[rows, :] = x_all[rows, :].astype(F32)
        if first:
            arrive(w4[0])
        out_part(rows, x)
        for k in (0, 2, 1):
            if first:
                arrive(w4[1 + k], send_a[k], send_a[3 + k])
            out_part(rows, lax.rem(x + 3 - k, XN))
        if first:
            ready(*ld_gu)
            ready(ld_d)
        stream = st[rows, :].astype(BF16).astype(F32)
        st[rows, :] = stream
        gate_up = dot(normed(stream).astype(BF16), wguv[...])
        gate = gate_up[:, :FF]
        hid[rows, :] = (gate / (1.0 + jnp.exp(-gate)) * gate_up[:, FF:]).astype(BF16)

    feed(yf, True)
    def down(half, cols):
        return dot(hid[half_rows(half), :], wdv[:, cols]).astype(BF16)

    def block(k):
        return pl.ds(pl.multiple_of(lax.rem(x + k, XN) * ROWS, ROWS), ROWS)

    pieces = [slice(c * (D // RC), (c + 1) * (D // RC)) for c in range(RC)]
    send_f = []
    for c, cols in enumerate(pieces):
        far[c] = down(yf, cols)
        for k in range(3):
            send_f.append(
                remote(RF + 3 * c + k, far.at[c, block(k + 1)], rf.at[c, k], xpeer(k + 1))
            )
            go(send_f[-1])
    feed(yh, False)
    near[...] = down(yh, slice(0, D))
    send_n = [remote(RN + k, near.at[block(k + 1)], rn.at[k], xpeer(k + 1)) for k in range(3)]
    go(*send_n)
    send_y = []
    for c in range(RC):
        total = far[c, block(0), :].astype(F32)
        for k in range(3):
            arrive(send_f[3 * c + k])
            total = total + rf[c, k].astype(F32)
        ys[c] = total.astype(BF16)
        send_y.append(remote(RY + c, ys.at[c], yr.at[c], ypeer))
        go(send_y[c])
    total = near[block(0), :].astype(F32)
    for k in range(3):
        arrive(send_n[k])
        total = total + rn[k].astype(F32)
    total = total + st[own_rows, :]
    for c, cols in enumerate(pieces):
        arrive(send_y[c])
        out[:, cols] = (total[:, cols] + yr[c].astype(F32)).astype(BF16)
    for copy in started:
        copy.wait_send()


def shards(
    tokens, variate, time_ids, cache_var, cache_len, linked, cache_kv, var_bias,
    w_qkv, w_out, w_gate_up, w_down,
):
    anyspace = pl.BlockSpec(memory_space=pltpu.HBM)
    smem = pl.BlockSpec(memory_space=pltpu.SMEM)
    vmem = pltpu.VMEM
    scratch = [
        vmem((TOK, D), BF16),
        vmem((D, 3 * HW), BF16),
        vmem((KEYS, 2 * HW), BF16),
        vmem((CACHE, HW), BF16),
        vmem((HW, KEYS), BF16),
        vmem((2, HW, HALF), BF16),
        vmem((2, 2 * HW, TOK), BF16),
        vmem((2, HW, HALF), BF16),
        vmem((2, 2 * HW, TOK), BF16),
        vmem((2, TOK), jnp.int32),
        vmem((2, TOK), jnp.int32),
        vmem((1, CACHE), jnp.int32),
        vmem((HD // 2, TOK), F32),
        vmem((HD // 2, TOK), F32),
        vmem((2, HD, TOK), BF16), vmem((8, TOK), F32),
        vmem((2, HD, TOK), BF16), vmem((8, TOK), F32),
        vmem((2, HD, TOK), BF16), vmem((8, TOK), F32),
        vmem((2, 2, HD, TOK), BF16), vmem((2, 8, TOK), F32),
        vmem((XN, 2, TOK, HW), BF16),
        vmem((XN, 2, 2, HD, D), BF16),
        vmem((D, 2 * FF), BF16),
        vmem((FF, D), BF16),
        vmem((TOK, D), F32),
        vmem((TOK, FF), BF16),
        vmem((RC, HALF, D // RC), BF16),
        vmem((HALF, D), BF16),
        vmem((RC, 3, ROWS, D // RC), BF16),
        vmem((3, ROWS, D), BF16),
        vmem((RC, ROWS, D // RC), BF16),
        vmem((RC, ROWS, D // RC), BF16),
        pltpu.SemaphoreType.DMA((NSEM,)),
        pltpu.SemaphoreType.DMA((NSEM,)),
        pltpu.SemaphoreType.DMA((14,)),
    ]
    return pl.pallas_call(
        layer,
        out_shape=pltpu.VMEM((ROWS, D), BF16),
        in_specs=[
            anyspace, anyspace, anyspace, anyspace, smem, smem, anyspace, smem,
            anyspace, anyspace, anyspace, anyspace,
        ],
        out_specs=pl.BlockSpec(memory_space=pltpu.VMEM),
        scratch_shapes=scratch,
        compiler_params=pltpu.CompilerParams(
            collective_id=0, has_side_effects=True, vmem_limit_bytes=60 << 20
        ),
        name="layer",
    )(
        tokens, time_ids.reshape(1, TOK), variate.reshape(1, TOK), cache_var.reshape(1, CACHE),
        cache_len, linked, cache_kv, var_bias, w_qkv, w_out, w_gate_up, w_down,
    )


def solution(mesh):
    return jax.shard_map(
        shards,
        mesh=mesh,
        in_specs=(
            P(("group", "tp"), None),
            P("group"),
            P("group"),
            P("group"),
            P("group"),
            P("group"),
            P(None, "group", "tp"),
            P(None, "tp"),
            P(None, None, "tp"),
            P("tp", None),
            P(None, None, "tp"),
            P("tp", None),
        ),
        out_specs=P(("group", "tp"), None),
        check_vma=False,
    )
```
